32 devices in a mesh: section: 8 (over z, core), ctx: 4 (over y, x).
Axes of the slice: x: 2, y: 2, z: 4, core: 2. Of those that a mesh axis runs over, the one named last changes fastest.
Arguments:
- activations: bfloat16 [8, 512, 5120], P('section', 'ctx'), may hold values from -6 to 6
- norm_gain: float32 [8, 5120], P('section'), may hold values from 0.5 to 1.5
- state_weight: bfloat16 [8, 5120, 256], P('section', 'ctx'), may hold values from -0.01953125 to 0.01953125
- step_weight: bfloat16 [8, 5120, 80], P('section', 'ctx'), may hold values from -0.078125 to 0.078125
- step_bias: float32 [8, 80], P('section'), may hold values from -5 to -3
- decay_log: float32 [8, 80], P('section'), may hold values from -6.4 to -0.2
- skip_gain: float32 [8, 80], P('section'), may hold values from 0.5 to 1.5
- carry_state: float32 [8, 80, 64, 128], P('section', 'ctx'), may hold values from -1.75 to 1.75
Outputs:
- handoff: bfloat16 [8, 512, 5120], P('section', 'ctx')
The draws below stay inside these ranges and needn't reach their ends.
All inputs are finite; a program needn't handle non-finite values.
Results may differ from the reference program's by a relative error of at most 0.006.
Values may be sent and summed in bfloat16 or wider, within the bound.
No kernel may reach another device: no remote copies, remote signals or barrier semaphores. Data moves between devices by JAX's collectives and lax.ppermute only.
A program may use at most 128 MiB of HBM per device.

```python
import jax
import jax.numpy as jnp
from jax import lax

D = 5120
HEADS = 80
HEAD_DIM = 64
STATE = 128
TOK_DEV = 128
SLAB = 512
LAYERS = 8
N_CTX = 4


def levels(rng, shape, pieces, smallest, high):
    loudness = 1.0
    for axis_at, parts in pieces:
        steps = jax.random.uniform(jax.random.fold_in(jax.random.fold_in(rng, 6), axis_at), (parts,), jnp.float32, smallest / len(pieces), high / len(pieces))
        loudness = loudness * jnp.repeat(jnp.exp(steps), shape[axis_at] // parts).reshape((-1,) + (1,) * (len(shape) - 1 - axis_at))
    return loudness


def centred(own_key, extent, spread, reach, shards=(), dtype=jnp.bfloat16):
    gain = levels(own_key, extent, shards, -0.22, 0.18) if shards else 1.0
    array = jax.random.normal(own_key, extent, jnp.float32) * spread * gain
    return jnp.minimum(jnp.maximum(array, -reach), reach).astype(dtype)


def setup_inputs(seed: int = 0) -> dict:
    key_list = jax.random.split(jax.random.key(seed), 9)
    return {
        "activations": centred(key_list[0], (LAYERS, SLAB, D), 1.0, 6.0, ((0, 8), (1, 4))),
        "norm_gain": jnp.clip(1.0 + 0.1 * jax.random.normal(key_list[1], (LAYERS, D), jnp.float32), 0.5, 1.5),
        "state_weight": centred(key_list[2], (LAYERS, D, 2 * STATE), (16 * D) ** -0.5, 0.01953125, ((0, 8), (1, 4))),
        "step_weight": centred(key_list[3], (LAYERS, D, HEADS), D ** -0.5, 0.078125, ((0, 8), (1, 4))),
        "step_bias": jnp.clip(-5.0 + 2.0 * jax.random.uniform(key_list[4], (LAYERS, HEADS), jnp.float32) ** levels(key_list[4], (LAYERS, HEADS), ((0, 8),), -0.2, 0.2), -5.0, -3.0),
        "decay_log": jnp.clip(-6.4 + 6.2000001 * jax.random.uniform(key_list[5], (LAYERS, HEADS), jnp.float32) ** levels(key_list[5], (LAYERS, HEADS), ((0, 8),), -0.2, 0.2), -6.4, -0.2),
        "skip_gain": jnp.clip(0.5 + 1.0 * jax.random.uniform(key_list[6], (LAYERS, HEADS), jnp.float32) ** levels(key_list[6], (LAYERS, HEADS), ((0, 8),), -0.2, 0.2), 0.5, 1.5),
        "carry_state": centred(key_list[7], (LAYERS, HEADS, HEAD_DIM, STATE), 0.3, 1.75, ((0, 8), (1, 4)), jnp.float32),
    }


EPS = 1e-05

def reference(activations, norm_gain, state_weight, step_weight, step_bias, decay_log, skip_gain, carry_state):

    def one_layer(packed):
        rows, gain_row, weight_bc, weight_step, bias_row, rate_log, skip_row, carry_row = packed
        inputs_f = rows.astype(jnp.float32)
        scale = lax.rsqrt(lax.optimization_barrier(jnp.mean(inputs_f * inputs_f, axis=1, keepdims=True)) + EPS)
        normed = (inputs_f * scale * gain_row).astype(jnp.bfloat16)
        projected = jnp.dot(normed, weight_bc, preferred_element_type=jnp.float32)
        b_rows = projected[:, :STATE].astype(jnp.bfloat16)
        c_rows = projected[:, STATE:].astype(jnp.bfloat16)
        raw_steps = jnp.dot(normed, weight_step, preferred_element_type=jnp.float32)
        step_size = jax.nn.softplus(raw_steps + bias_row)
        log_decay = -step_size * jnp.exp(rate_log)
        shaped = (normed.reshape(N_CTX, TOK_DEV, HEADS, HEAD_DIM), b_rows.reshape(N_CTX, TOK_DEV, STATE), c_rows.reshape(N_CTX, TOK_DEV, STATE), step_size.reshape(N_CTX, TOK_DEV, HEADS), log_decay.reshape(N_CTX, TOK_DEV, HEADS), inputs_f.reshape(N_CTX, TOK_DEV, D))
        causal = jnp.arange(TOK_DEV)[:, None] >= jnp.arange(TOK_DEV)[None, :]

        def advance(state, block):
            heads_x, b_blk, c_blk, steps_blk, decay_blk, inputs_blk = block
            cumulative = jnp.cumsum(decay_blk, axis=0)
            by_head = cumulative.T
            gap = by_head[:, :, None] - by_head[:, None, :]
            factor = jnp.where(causal[None], jnp.exp(jnp.where(causal[None], gap, 0.0)), 0.0)
            scores = jnp.dot(c_blk, b_blk.T, preferred_element_type=jnp.float32)
            mixing = (factor * scores[None] * steps_blk.T[:, None, :]).astype(jnp.bfloat16)
            intra = jnp.einsum('hts,shp->thp', mixing.astype(jnp.float32), heads_x.astype(jnp.float32))
            tail = jnp.exp(cumulative[-1][None, :] - cumulative) * steps_blk
            weighted = (heads_x.astype(jnp.float32) * tail[:, :, None]).astype(jnp.bfloat16)
            block_state = jnp.einsum('shp,sn->hpn', weighted.astype(jnp.float32), b_blk.astype(jnp.float32))
            start_low = state.astype(jnp.bfloat16)
            inter = jnp.exp(cumulative)[:, :, None] * jnp.einsum('tn,hpn->thp', c_blk.astype(jnp.float32), start_low.astype(jnp.float32))
            mixed = intra + inter + skip_row[None, :, None] * heads_x.astype(jnp.float32)
            output = (inputs_blk + mixed.reshape(TOK_DEV, D)).astype(jnp.bfloat16)
            new_state = jnp.exp(cumulative[-1])[:, None, None] * state + block_state
            return (new_state, output)
        final_state, outputs = lax.scan(advance, carry_row, shaped)
        return outputs.reshape(SLAB, D)
    results = lax.map(one_layer, (activations, norm_gain, state_weight, step_weight, step_bias, decay_log, skip_gain, carry_state))
    return jnp.roll(results, 1, axis=0)
```

```python
import functools

import jax
import jax.numpy as jnp
from jax import lax
from jax.experimental import pallas as pl
from jax.experimental.pallas import tpu as pltpu
from jax.sharding import PartitionSpec as P

HEAD_DIM = 64
STATE = 128
EPS = 1e-05
GROUP = 32
VMEM_LIMIT = 24 << 20

F32, BF16 = jnp.float32, jnp.bfloat16


def entering(shard, axis, combine, identity):
    count, place = (lax.axis_size(axis), lax.axis_index(axis))
    everything = jax.tree.map(
        lambda part, kind: lax.all_gather(part.astype(kind), axis), shard, (BF16, BF16)
    )
    start = jax.tree.map(
        lambda part, zero: jnp.broadcast_to(jnp.asarray(zero, part.dtype), part.shape),
        shard,
        identity,
    )

    def lap(k, before):
        reached = k < place
        new = combine(
            before, jax.tree.map(lambda part, own: part[k].astype(own.dtype), everything, shard)
        )
        return jax.tree.map(lambda a, b: jnp.where(reached, a, b), new, before)

    return lax.fori_loop(0, count, lap, start)


def combine_states(earlier, later):
    return (earlier[0] + later[0], jnp.exp(later[0])[:, None, None] * earlier[1] + later[1])


def by_positions(
    activations, norm_gain, state_weight, step_weight, step_bias, decay_log, skip_gain, carry_state
):
    rows = activations[0]
    count = rows.shape[0]
    heads = step_weight.shape[2]
    inputs_f = rows.astype(F32)
    scale = lax.rsqrt(jnp.mean(inputs_f * inputs_f, axis=1, keepdims=True) + EPS)
    normed = (inputs_f * scale * norm_gain[0]).astype(BF16)
    first = jnp.dot(
        normed,
        lax.all_gather(state_weight, "ctx", axis=1, tiled=True)[0],
        preferred_element_type=F32,
    )
    second = jnp.dot(
        normed,
        lax.all_gather(step_weight, "ctx", axis=1, tiled=True)[0],
        preferred_element_type=F32,
    )
    b_rows = first[:, :STATE].astype(BF16)
    c_rows = first[:, STATE:].astype(BF16)
    step_size = jax.nn.softplus(second + step_bias[0])
    log_decay = -step_size * jnp.exp(decay_log[0])
    heads_x = normed.reshape(count, heads, HEAD_DIM)
    causal = jnp.arange(count)[:, None] >= jnp.arange(count)[None, :]
    cumulative = jnp.dot(causal.astype(F32), log_decay, precision=lax.Precision.HIGHEST)
    by_head = cumulative.T
    gap = by_head[:, :, None] - by_head[:, None, :]
    factor = jnp.where(causal[None], jnp.exp(jnp.where(causal[None], gap, 0.0)), 0.0)
    scores = jnp.dot(c_rows, b_rows.T, preferred_element_type=F32)
    mixing = (factor * scores[None] * step_size.T[:, None, :]).astype(BF16)
    intra = jnp.einsum("hts,shp->thp", mixing, heads_x, preferred_element_type=F32)
    tail = jnp.exp(cumulative[-1][None, :] - cumulative) * step_size
    weighted = (heads_x.astype(F32) * tail[:, :, None]).astype(BF16)
    block_state = jnp.einsum("shp,sn->hpn", weighted, b_rows, preferred_element_type=F32)
    carry_full = lax.all_gather(carry_state[0].astype(BF16), "ctx", axis=0, tiled=True).astype(F32)
    identity = (jnp.zeros((heads,), F32), jnp.zeros(block_state.shape, F32))
    prefix_decay, prefix_state = entering(
        (cumulative[-1], block_state), "ctx", combine_states, identity
    )
    start = jnp.exp(prefix_decay)[:, None, None] * carry_full + prefix_state
    inter = jnp.exp(cumulative)[:, :, None] * jnp.einsum(
        "tn,hpn->thp", c_rows, start.astype(BF16), preferred_element_type=F32
    )
    mixed = intra + inter + skip_gain[0][None, :, None] * heads_x.astype(F32)
    output = (inputs_f + mixed.reshape(count, heads * HEAD_DIM)).astype(BF16)
    sections = lax.axis_size("section")
    route = [(i, (i + 1) % sections) for i in range(sections)]
    return lax.ppermute(output[None], "section", route)


def params(**more):
    return pltpu.CompilerParams(vmem_limit_bytes=VMEM_LIMIT, **more)


def split_kernel(me_ref, x_ref, *refs):
    outs, sems = refs[:-1], refs[-1]
    columns = outs[0].shape[1]
    me = me_ref[0]
    copies = []
    for d, out in enumerate(outs, 1):
        at = pl.multiple_of(lax.bitwise_xor(me, d) * columns, 128)
        copies.append(
            pltpu.make_async_copy(x_ref.at[:, pl.ds(at, columns)], out, sems.at[d - 1])
        )
    for copy in copies:
        copy.start()
    for copy in copies:
        copy.wait()


def split(me, rows, columns):
    count = rows.shape[0]
    return pl.pallas_call(
        split_kernel,
        out_shape=[jax.ShapeDtypeStruct((count, columns), BF16)] * 3,
        grid_spec=pltpu.PrefetchScalarGridSpec(
            num_scalar_prefetch=1,
            grid=(1,),
            in_specs=[pl.BlockSpec(memory_space=pl.ANY)],
            out_specs=[pl.BlockSpec(memory_space=pl.ANY)] * 3,
            scratch_shapes=[pltpu.SemaphoreType.DMA((3,))],
        ),
        compiler_params=params(),
        name="split",
    )(me, rows)


def join_kernel(me_ref, *refs):
    parts, out, sems = refs[:-2], refs[-2], refs[-1]
    columns = parts[0].shape[1]
    me = me_ref[0]
    copies = []
    for d, part in enumerate(parts):
        at = pl.multiple_of(lax.bitwise_xor(me, d) * columns, 128)
        copies.append(pltpu.make_async_copy(part, out.at[:, pl.ds(at, columns)], sems.at[d]))
    for copy in copies:
        copy.start()
    for copy in copies:
        copy.wait()


def join(me, parts):
    count, columns = parts[0].shape
    return pl.pallas_call(
        join_kernel,
        out_shape=jax.ShapeDtypeStruct((count, columns * 4), BF16),
        grid_spec=pltpu.PrefetchScalarGridSpec(
            num_scalar_prefetch=1,
            grid=(1,),
            in_specs=[pl.BlockSpec(memory_space=pl.ANY)] * 4,
            out_specs=pl.BlockSpec(memory_space=pl.ANY),
            scratch_shapes=[pltpu.SemaphoreType.DMA((4,))],
        ),
        compiler_params=params(),
        name="join",
    )(me, *parts)


def lanes_of(shape):
    return lax.broadcasted_iota(jnp.int32, shape, 1)


def partial_kernel(heads, me_ref, x0, x1, x2, x3, gain_ref, w_ref, ws_ref, *outs):
    count = x0.shape[0]
    gain = gain_ref[...]
    lane = lanes_of((count, 128))
    steps = [jnp.zeros((count, 128), F32) for _ in range(4)]
    for e, x_ref in enumerate((x0, x1, x2, x3)):
        x = x_ref[...].astype(F32)
        squares = jnp.sum(x * x, axis=1, keepdims=True)
        scaled = (x * gain).astype(BF16)
        rows = jnp.dot(scaled, w_ref[...], preferred_element_type=F32).astype(BF16)
        raw = jnp.dot(scaled, ws_ref[...], preferred_element_type=F32)
        for d in range(4):
            to = e ^ d
            outs[d][to * count : (to + 1) * count, :] = rows
            moved = pltpu.roll(raw, (to - d) * GROUP % 128, 1) if to != d else raw
            here = (lane >= to * GROUP) & (lane < to * GROUP + heads)
            steps[d] = jnp.where(here, moved, steps[d])
            steps[d] = jnp.where(lane == to * GROUP + heads, squares, steps[d])
    for d in range(4):
        high = steps[d].astype(BF16)
        low = (steps[d] - high.astype(F32)).astype(BF16)
        outs[d][4 * count :, :128] = high
        outs[d][4 * count :, 128:] = low


def own_columns(count, columns):
    return pl.BlockSpec((count, columns), lambda i, me: (0, me[0]))


def partials(me, rows, received, gain, weight, step_weight, heads):
    count, columns = received[0].shape
    full = lambda a: pl.BlockSpec(a.shape, lambda i, me: (0,) * a.ndim)
    return pl.pallas_call(
        functools.partial(partial_kernel, heads),
        out_shape=[jax.ShapeDtypeStruct((5 * count, 2 * STATE), BF16)] * 4,
        grid_spec=pltpu.PrefetchScalarGridSpec(
            num_scalar_prefetch=1,
            grid=(1,),
            in_specs=[
                own_columns(count, columns),
                *[full(r) for r in received],
                own_columns(1, columns),
                full(weight),
                full(step_weight),
            ],
            out_specs=[pl.BlockSpec((5 * count, 2 * STATE), lambda i, me: (0, 0))] * 4,
        ),
        compiler_params=params(),
        name="partials",
    )(me, rows, *received, gain, weight, step_weight)


def by_pair(values, column, lane):
    left = jnp.broadcast_to(values[:, column : column + 1], lane.shape)
    right = jnp.broadcast_to(values[:, column + 1 : column + 2], lane.shape)
    return jnp.where(lane < HEAD_DIM, left, right)


def states_kernel(
    heads, width, me_ref, x0, x1, x2, x3, p0, p1, p2, p3, gain_ref, vec_ref, carry_ref,
    bc_ref, cum_ref, cumt_ref, stept_ref, start_ref, made, kept,
):
    count, columns = x0.shape
    me = me_ref[0]
    lane = lanes_of((count, 128))
    payloads = (p0, p1, p2, p3)
    raw = jnp.zeros((count, 128), F32)
    for p in payloads:
        raw += p[4 * count :, :128].astype(F32) + p[4 * count :, 128:].astype(F32)
    scales = []
    for e in range(4):
        at = e * GROUP + heads
        squares = jnp.broadcast_to(raw[:, at : at + 1], (count, 128))
        scales.append(lax.rsqrt(squares * (1.0 / width) + EPS))
    scale = scales[0]
    for e in range(1, 4):
        scale = jnp.where(lane >= e * GROUP, scales[e], scale)
    biased = raw * scale + vec_ref[0:1, :]
    step = jnp.maximum(biased, 0.0) + jnp.log1p(jnp.exp(-jnp.abs(biased)))
    step = jnp.where(lane % GROUP < heads, step, 0.0)
    log_decay = step * vec_ref[1:2, :]
    lower = lax.broadcasted_iota(jnp.int32, (count, count), 0) >= lax.broadcasted_iota(
        jnp.int32, (count, count), 1
    )
    cum = jnp.dot(
        lower.astype(F32),
        log_decay,
        precision=lax.Precision.HIGHEST,
        preferred_element_type=F32,
    )
    last = cum[count - 1 : count, :]
    tail = jnp.exp(last - cum) * step
    decay = jnp.exp(last)
    cum_ref[...] = jnp.where(lane % GROUP == heads, scale, cum)
    cumt_ref[...] = cum.T
    stept_ref[...] = step.T
    for e, x_ref in enumerate((x0, x1, x2, x3)):
        rows = sum(p[e * count : (e + 1) * count, :].astype(F32) for p in payloads)
        both = jnp.concatenate(
            [rows[:, :128] * scales[e], rows[:, 128:] * scales[e]], axis=1
        ).astype(BF16)
        bc_ref[e] = both
        b_turned = both[:, :128].astype(F32).T.astype(BF16)
        block = lax.bitwise_xor(me, e)
        for j in range(columns // 128):
            at = slice(j * 128, (j + 1) * 128)
            column = e * GROUP + 2 * j
            x = x_ref[:, at].astype(F32)
            normed = (x * scales[e] * gain_ref[:, at]).astype(BF16).astype(F32)
            weighted = (normed * by_pair(tail, column, lane)).astype(BF16)
            made[block, :, at] = jnp.dot(b_turned, weighted, preferred_element_type=F32)
            kept[block, :, at] = by_pair(
                jnp.broadcast_to(decay, (8, 128)), column, lane[:8]
            )
    for j in range(columns // 128):
        at = slice(j * 128, (j + 1) * 128)
        state = carry_ref[:, at]
        for t in range(4):
            start_ref[lax.bitwise_xor(me, t), :, at] = state.astype(BF16)
            if t < 3:
                state = kept[t, 0:1, at] * state + made[t, :, at]


def states(me, rows, received, payloads, gain, vectors, carry, heads):
    count, columns = received[0].shape
    full = lambda shape: pl.BlockSpec(shape, lambda i, me: (0,) * len(shape))
    outs = [
        ((4, count, 2 * STATE), BF16),
        ((count, 128), F32),
        ((128, count), F32),
        ((128, count), F32),
        ((4, STATE, columns), BF16),
    ]
    return pl.pallas_call(
        functools.partial(states_kernel, heads, rows.shape[1]),
        out_shape=[jax.ShapeDtypeStruct(*o) for o in outs],
        grid_spec=pltpu.PrefetchScalarGridSpec(
            num_scalar_prefetch=1,
            grid=(1,),
            in_specs=[
                own_columns(count, columns),
                *[full(r.shape) for r in received],
                *[full(p.shape) for p in payloads],
                own_columns(1, columns),
                full(vectors.shape),
                full(carry.shape),
            ],
            out_specs=[full(o[0]) for o in outs],
            scratch_shapes=[
                pltpu.VMEM((4, STATE, columns), F32),
                pltpu.VMEM((4, 8, columns), F32),
            ],
        ),
        compiler_params=params(),
        name="states",
    )(me, rows, *received, *payloads, gain, vectors, carry)


def output_kernel(
    heads, e, me_ref, x_ref, bc_ref, cum_ref, cumt_ref, stept_ref, start_ref, gain_ref, skip_ref,
    out_ref,
):
    count, columns = x_ref.shape
    lane = lanes_of((count, 128))
    b_rows, c_rows = bc_ref[0, :, :128], bc_ref[0, :, 128:]
    cum = cum_ref[...]
    grown = jnp.exp(cum)
    at = e * GROUP + heads
    scale = jnp.broadcast_to(cum[:, at : at + 1], (count, 128))
    lower = lax.broadcasted_iota(jnp.int32, (count, count), 0) >= lax.broadcasted_iota(
        jnp.int32, (count, count), 1
    )
    scores = lax.dot_general(
        c_rows, b_rows, (((1,), (1,)), ((), ())), preferred_element_type=F32
    )
    scores = jnp.where(lower, scores, 0.0)
    for j in range(columns // 128):
        at = slice(j * 128, (j + 1) * 128)
        x = x_ref[:, at].astype(F32)
        low = (x * scale * gain_ref[:, at]).astype(BF16)
        normed = low.astype(F32)
        mixing, spread = [], []
        for k in range(2):
            column = e * GROUP + 2 * j + k
            row = 2 * j + k
            gap = cum[:, column : column + 1] - cumt_ref[row : row + 1, :]
            factor = jnp.exp(jnp.where(lower, gap, 0.0))
            mixing.append((factor * scores * stept_ref[row : row + 1, :]).astype(BF16))
            mine = (lane < HEAD_DIM) if k == 0 else (lane >= HEAD_DIM)
            spread.append(jnp.where(mine, normed, 0.0).astype(BF16))
        intra = jnp.dot(
            jnp.concatenate(mixing, axis=1),
            jnp.concatenate(spread, axis=0),
            preferred_element_type=F32,
        )
        inter = jnp.dot(c_rows, start_ref[0, :, at], preferred_element_type=F32)
        inter = by_pair(grown, e * GROUP + 2 * j, lane) * inter
        mixed = intra + inter + skip_ref[:, at] * normed
        out_ref[:, at] = (x + mixed).astype(BF16)


def output_block(e, me, x, made, gain, skip, heads):
    bc, cum, cumt, stept, start = made
    count = bc.shape[1]
    columns = start.shape[2]
    full = lambda shape: pl.BlockSpec(shape, lambda i, me: (0,) * len(shape))
    return pl.pallas_call(
        functools.partial(output_kernel, heads, e),
        out_shape=jax.ShapeDtypeStruct((count, columns), BF16),
        grid_spec=pltpu.PrefetchScalarGridSpec(
            num_scalar_prefetch=1,
            grid=(1,),
            in_specs=[
                own_columns(count, columns) if e == 0 else full(x.shape),
                pl.BlockSpec((1, count, 2 * STATE), lambda i, me: (e, 0, 0)),
                full(cum.shape),
                pl.BlockSpec((GROUP, count), lambda i, me: (e, 0)),
                pl.BlockSpec((GROUP, count), lambda i, me: (e, 0)),
                pl.BlockSpec((1, STATE, columns), lambda i, me: (e, 0, 0)),
                own_columns(1, columns),
                full(skip.shape),
            ],
            out_specs=pl.BlockSpec((count, columns), lambda i, me: (0, 0)),
        ),
        compiler_params=params(),
        name=f"output_{e}",
    )(me, x, bc, cum, cumt, stept, start, gain, skip)


def by_heads(
    activations, norm_gain, state_weight, step_weight, step_bias, decay_log, skip_gain, carry_state
):
    rows = activations[0]
    heads = carry_state.shape[1]
    columns = heads * HEAD_DIM
    here = lax.axis_index("ctx")
    me = here.astype(jnp.int32).reshape(1)
    sections = lax.axis_size("section")

    sent = split(me, rows, columns)
    received = [
        lax.ppermute(part, "ctx", [(i, i ^ d) for i in range(4)]) for d, part in enumerate(sent, 1)
    ]

    pad = lambda a: jnp.pad(a, ((0, 0),) * (a.ndim - 1) + ((0, GROUP - heads),))
    ours = lambda a, d: lax.dynamic_slice_in_dim(a, (here ^ d) * heads, heads, a.ndim - 1)
    spread_steps = jnp.concatenate([pad(ours(step_weight[0], d)) for d in range(4)], axis=1)
    payloads = partials(me, rows, received, norm_gain, state_weight[0], spread_steps, heads)
    payloads = [payloads[0]] + [
        lax.ppermute(part, "ctx", [(i, i ^ d) for i in range(4)])
        for d, part in enumerate(payloads[1:], 1)
    ]

    vectors = jnp.concatenate(
        [
            jnp.tile(pad(ours(step_bias, 0)), (1, 4)),
            jnp.tile(pad(-jnp.exp(ours(decay_log, 0))), (1, 4)),
            jnp.zeros((6, 4 * GROUP), F32),
        ]
    )
    skip = jnp.repeat(ours(skip_gain, 0), HEAD_DIM, axis=1)
    carry = carry_state[0].reshape(columns, STATE).T
    made = states(me, rows, received, payloads, norm_gain, vectors, carry, heads)

    parts = {}
    for d in (3, 1, 2, 0):
        x = rows if d == 0 else received[d - 1]
        block = output_block(d, me, x, made, norm_gain, skip, heads)
        route = [
            (s * 4 + c, ((s + 1) % sections) * 4 + (c ^ d))
            for s in range(sections)
            for c in range(4)
        ]
        parts[d] = lax.ppermute(block, ("section", "ctx"), route)
    return join(me, [parts[d] for d in range(4)])[None]


def per_device(*arguments):
    activations, carry_state = arguments[0], arguments[-1]
    heads, dim, state = carry_state.shape[1:]
    fits = (
        lax.axis_size("ctx") == 4
        and activations.shape[1] == 128
        and (dim, state) == (HEAD_DIM, STATE)
        and heads % 2 == 0
        and heads < GROUP
    )
    return (by_heads if fits else by_positions)(*arguments)


def solution(mesh):
    placed = (
        P("section", "ctx", None),
        P("section", None),
        P("section", "ctx", None),
        P("section", "ctx", None),
        P("section", None),
        P("section", None),
        P("section", None),
        P("section", "ctx", None, None),
    )
    return jax.shard_map(
        per_device, mesh=mesh, in_specs=placed, out_specs=P("section", "ctx", None), check_vma=False
    )
```

```python
import functools
import math

import jax
import jax.numpy as jnp
from jax import lax
from jax.experimental import pallas as pl
from jax.experimental.pallas import tpu as pltpu
from jax.sharding import PartitionSpec as P

HEAD_DIM = 64
STATE = 128
EPS = 1e-05
GROUP = 32
VMEM_LIMIT = 24 << 20
CUTS = 4
ORDER = (3, 1, 2, 0)
OUTPUT_FLOPS = 2 * 128 * 1280 * 384

F32, BF16 = jnp.float32, jnp.bfloat16


def entering(shard, axis, combine, identity):
    count, place = (lax.axis_size(axis), lax.axis_index(axis))
    everything = jax.tree.map(
        lambda part, kind: lax.all_gather(part.astype(kind), axis), shard, (BF16, BF16)
    )
    start = jax.tree.map(
        lambda part, zero: jnp.broadcast_to(jnp.asarray(zero, part.dtype), part.shape),
        shard,
        identity,
    )

    def lap(k, before):
        reached = k < place
        new = combine(
            before, jax.tree.map(lambda part, own: part[k].astype(own.dtype), everything, shard)
        )
        return jax.tree.map(lambda a, b: jnp.where(reached, a, b), new, before)

    return lax.fori_loop(0, count, lap, start)


def combine_states(earlier, later):
    return (earlier[0] + later[0], jnp.exp(later[0])[:, None, None] * earlier[1] + later[1])


def by_positions(
    activations, norm_gain, state_weight, step_weight, step_bias, decay_log, skip_gain, carry_state
):
    rows = activations[0]
    count = rows.shape[0]
    heads = step_weight.shape[2]
    inputs_f = rows.astype(F32)
    scale = lax.rsqrt(jnp.mean(inputs_f * inputs_f, axis=1, keepdims=True) + EPS)
    normed = (inputs_f * scale * norm_gain[0]).astype(BF16)
    first = jnp.dot(
        normed,
        lax.all_gather(state_weight, "ctx", axis=1, tiled=True)[0],
        preferred_element_type=F32,
    )
    second = jnp.dot(
        normed,
        lax.all_gather(step_weight, "ctx", axis=1, tiled=True)[0],
        preferred_element_type=F32,
    )
    b_rows = first[:, :STATE].astype(BF16)
    c_rows = first[:, STATE:].astype(BF16)
    step_size = jax.nn.softplus(second + step_bias[0])
    log_decay = -step_size * jnp.exp(decay_log[0])
    heads_x = normed.reshape(count, heads, HEAD_DIM)
    causal = jnp.arange(count)[:, None] >= jnp.arange(count)[None, :]
    cumulative = jnp.dot(causal.astype(F32), log_decay, precision=lax.Precision.HIGHEST)
    by_head = cumulative.T
    gap = by_head[:, :, None] - by_head[:, None, :]
    factor = jnp.where(causal[None], jnp.exp(jnp.where(causal[None], gap, 0.0)), 0.0)
    scores = jnp.dot(c_rows, b_rows.T, preferred_element_type=F32)
    mixing = (factor * scores[None] * step_size.T[:, None, :]).astype(BF16)
    intra = jnp.einsum("hts,shp->thp", mixing, heads_x, preferred_element_type=F32)
    tail = jnp.exp(cumulative[-1][None, :] - cumulative) * step_size
    weighted = (heads_x.astype(F32) * tail[:, :, None]).astype(BF16)
    block_state = jnp.einsum("shp,sn->hpn", weighted, b_rows, preferred_element_type=F32)
    carry_full = lax.all_gather(carry_state[0].astype(BF16), "ctx", axis=0, tiled=True).astype(F32)
    identity = (jnp.zeros((heads,), F32), jnp.zeros(block_state.shape, F32))
    prefix_decay, prefix_state = entering(
        (cumulative[-1], block_state), "ctx", combine_states, identity
    )
    start = jnp.exp(prefix_decay)[:, None, None] * carry_full + prefix_state
    inter = jnp.exp(cumulative)[:, :, None] * jnp.einsum(
        "tn,hpn->thp", c_rows, start.astype(BF16), preferred_element_type=F32
    )
    mixed = intra + inter + skip_gain[0][None, :, None] * heads_x.astype(F32)
    output = (inputs_f + mixed.reshape(count, heads * HEAD_DIM)).astype(BF16)
    sections = lax.axis_size("section")
    route = [(i, (i + 1) % sections) for i in range(sections)]
    return lax.ppermute(output[None], "section", route)


def params():
    return pltpu.CompilerParams(vmem_limit_bytes=VMEM_LIMIT)


def call(kernel, name, outs, scratch=(), where=pltpu.VMEM, source=pltpu.VMEM, flops=0):
    def run(me, *arrays):
        results = pl.pallas_call(
            kernel,
            out_shape=[jax.ShapeDtypeStruct(*o) for o in outs],
            in_specs=[pl.BlockSpec(memory_space=pltpu.SMEM)]
            + [pl.BlockSpec(memory_space=source)] * len(arrays),
            out_specs=[pl.BlockSpec(memory_space=where)] * len(outs),
            scratch_shapes=scratch,
            compiler_params=params(),
            cost_estimate=pl.CostEstimate(
                flops=flops,
                transcendentals=0,
                bytes_accessed=sum(a.size * a.dtype.itemsize for a in arrays)
                + sum(math.prod(shape) * jnp.dtype(kind).itemsize for shape, kind in outs),
            ),
            name=name,
        )(me, *arrays)
        return list(results)

    return run


def split_kernel(me_ref, x_ref, *refs):
    outs, sems = refs[:-1], refs[-1]
    count, columns = outs[0].shape
    me = me_ref[0]
    copies = []
    for d, out in enumerate(outs):
        at = pl.multiple_of(lax.bitwise_xor(me, d) * columns, 128)
        for k in range(CUTS):
            part = slice(k * count // CUTS, (k + 1) * count // CUTS)
            copies.append(
                pltpu.make_async_copy(
                    x_ref.at[part, pl.ds(at, columns)], out.at[part], sems.at[d * CUTS + k]
                )
            )
    for copy in copies:
        copy.start()
    for copy in copies:
        copy.wait()


def join_kernel(me_ref, *refs):
    parts, out, sems = refs[:-2], refs[-2], refs[-1]
    count, columns = parts[0].shape
    me = me_ref[0]
    copies = []
    for d, block in enumerate(parts):
        at = pl.multiple_of(lax.bitwise_xor(me, d) * columns, 128)
        for k in range(CUTS):
            part = slice(k * count // CUTS, (k + 1) * count // CUTS)
            copies.append(
                pltpu.make_async_copy(
                    block.at[part], out.at[part, pl.ds(at, columns)], sems.at[d * CUTS + k]
                )
            )
    for copy in copies:
        copy.start()
    for copy in copies:
        copy.wait()


def lanes_of(shape):
    return lax.broadcasted_iota(jnp.int32, shape, 1)


def partial_kernel(heads, _, x_ref, gain_ref, w_ref, ws_ref, out_ref):
    x = x_ref[...].astype(F32)
    squares = jnp.sum(x * x, axis=1, keepdims=True)
    high = squares.astype(BF16).astype(F32)
    scaled = (x * gain_ref[...]).astype(BF16)
    rows = jnp.dot(scaled, w_ref[...], preferred_element_type=F32)
    raw = lax.dot_general(scaled, ws_ref[...], (((1,), (1,)), ((), ())), preferred_element_type=F32)
    lane = lanes_of(raw.shape)
    raw = jnp.where(lane == heads, high, raw)
    raw = jnp.where(lane == heads + 1, squares - high, raw)
    out_ref[:, : 2 * STATE] = rows.astype(BF16)
    out_ref[:, 2 * STATE :] = raw.astype(BF16)


def total_kernel(
    heads, width, me_ref, p0, p1, p2, p3, bias_ref, o0, o1, o2, o3, turned
):
    count = p0.shape[0]
    me = me_ref[0]
    total = sum(p[...].astype(F32) for p in (p0, p1, p2, p3))
    rows, raw = total[:, : 2 * STATE], total[:, 2 * STATE :]
    lane = lanes_of(raw.shape)
    squares = raw[:, heads : heads + 1] + raw[:, heads + 1 : heads + 2]
    scale = lax.rsqrt(jnp.broadcast_to(squares, raw.shape) * (1.0 / width) + EPS)
    biased = raw * scale + bias_ref[...]
    step = jnp.maximum(biased, 0.0) + jnp.log1p(jnp.exp(-jnp.abs(biased)))
    step = jnp.where(lane % GROUP == heads, scale, step)
    step = jnp.where(lane % GROUP > heads, 0.0, step)
    by_head = step.T
    high = by_head.astype(BF16)
    turned[:, :count] = high
    turned[:, count:] = (by_head - high.astype(F32)).astype(BF16)
    both = jnp.concatenate([rows[:, :STATE] * scale, rows[:, STATE:] * scale], axis=1).astype(BF16)
    for d, out in enumerate((o0, o1, o2, o3)):
        at = pl.multiple_of(lax.bitwise_xor(me, d) * GROUP, GROUP)
        out[:count, :] = both
        out[count:, :] = turned[pl.ds(at, GROUP), :]


def by_pair(values, column, lane):
    left = jnp.broadcast_to(values[:, column : column + 1], lane.shape)
    right = jnp.broadcast_to(values[:, column + 1 : column + 2], lane.shape)
    return jnp.where(lane < HEAD_DIM, left, right)


def states_kernel(
    heads, me_ref, x0, x1, x2, x3, p0, p1, p2, p3, gain_ref, rate_ref, carry_ref,
    cum_ref, cumt_ref, stept_ref, start_ref, made, kept,
):
    count, columns = x0.shape
    me = me_ref[0]
    lane = lanes_of((count, 128))
    payloads = (p0, p1, p2, p3)
    by_head = jnp.concatenate(
        [p[count:, :count].astype(F32) + p[count:, count:].astype(F32) for p in payloads]
    )
    stept_ref[...] = by_head
    step = by_head.T
    log_decay = step * rate_ref[...]
    lower = lax.broadcasted_iota(jnp.int32, (count, count), 0) >= lax.broadcasted_iota(
        jnp.int32, (count, count), 1
    )
    cum = jnp.dot(
        lower.astype(F32),
        log_decay,
        precision=lax.Precision.HIGHEST,
        preferred_element_type=F32,
    )
    last = cum[count - 1 : count, :]
    tail = jnp.exp(last - cum) * step
    decay = jnp.exp(last)
    cum_ref[...] = jnp.where(lane % GROUP == heads, step, cum)
    cumt_ref[...] = cum.T
    for e, x_ref in enumerate((x0, x1, x2, x3)):
        b_turned = payloads[e][:count, :STATE].astype(F32).T.astype(BF16)
        at = e * GROUP + heads
        scale = jnp.broadcast_to(step[:, at : at + 1], (count, 128))
        block = lax.bitwise_xor(me, e)
        for j in range(columns // 128):
            at = slice(j * 128, (j + 1) * 128)
            column = e * GROUP + 2 * j
            x = x_ref[:, at].astype(F32)
            normed = (x * scale * gain_ref[:, at]).astype(BF16).astype(F32)
            weighted = (normed * by_pair(tail, column, lane)).astype(BF16)
            made[block, :, at] = jnp.dot(b_turned, weighted, preferred_element_type=F32)
            kept[block, :, at] = by_pair(
                jnp.broadcast_to(decay, (8, 128)), column, lane[:8]
            )
    for j in range(columns // 128):
        at = slice(j * 128, (j + 1) * 128)
        state = carry_ref[:, at]
        for t in range(4):
            start_ref[lax.bitwise_xor(me, t), :, at] = state.astype(BF16)
            if t < 3:
                state = kept[t, 0:1, at] * state + made[t, :, at]


def output_kernel(
    heads, e, _, x_ref, payload_ref, cum_ref, cumt_ref, stept_ref, start_ref, gain_ref, skip_ref,
    out_ref,
):
    count, columns = x_ref.shape
    lane = lanes_of((count, 128))
    b_rows, c_rows = payload_ref[:count, :STATE], payload_ref[:count, STATE:]
    cum = cum_ref[...]
    grown = jnp.exp(cum)
    at = e * GROUP + heads
    scale = jnp.broadcast_to(cum[:, at : at + 1], (count, 128))
    lower = lax.broadcasted_iota(jnp.int32, (count, count), 0) >= lax.broadcasted_iota(
        jnp.int32, (count, count), 1
    )
    scores = lax.dot_general(
        c_rows, b_rows, (((1,), (1,)), ((), ())), preferred_element_type=F32
    )
    scores = jnp.where(lower, scores, 0.0)
    for j in range(columns // 128):
        at = slice(j * 128, (j + 1) * 128)
        x = x_ref[:, at].astype(F32)
        low = (x * scale * gain_ref[:, at]).astype(BF16)
        normed = low.astype(F32)
        mixing, spread = [], []
        for k in range(2):
            column = e * GROUP + 2 * j + k
            row = column
            gap = cum[:, column : column + 1] - cumt_ref[row : row + 1, :]
            factor = jnp.exp(jnp.where(lower, gap, 0.0))
            mixing.append((factor * scores * stept_ref[row : row + 1, :]).astype(BF16))
            mine = (lane < HEAD_DIM) if k == 0 else (lane >= HEAD_DIM)
            spread.append(jnp.where(mine, normed, 0.0).astype(BF16))
        intra = jnp.dot(
            jnp.concatenate(mixing, axis=1),
            jnp.concatenate(spread, axis=0),
            preferred_element_type=F32,
        )
        inter = jnp.dot(c_rows, start_ref[e, :, at], preferred_element_type=F32)
        inter = by_pair(grown, e * GROUP + 2 * j, lane) * inter
        mixed = intra + inter + skip_ref[:, at] * normed
        out_ref[:, at] = (x + mixed).astype(BF16)


def by_heads(
    activations, norm_gain, state_weight, step_weight, step_bias, decay_log, skip_gain, carry_state
):
    rows = activations[0]
    count, width = rows.shape
    heads = carry_state.shape[1]
    columns = heads * HEAD_DIM
    here = lax.axis_index("ctx")
    me = here.astype(jnp.int32).reshape(1)
    sections = lax.axis_size("section")
    block = ((count, columns), BF16)

    x = call(
        split_kernel,
        "split",
        [block] * 4,
        [pltpu.SemaphoreType.DMA((4 * CUTS,))],
        source=pl.ANY,
    )(me, pltpu.with_memory_space_constraint(rows, pltpu.HBM))
    x[1:] = [
        lax.ppermute(part, "ctx", [(i, i ^ d) for i in range(4)]) for d, part in enumerate(x[1:], 1)
    ]

    grouped = lambda a: jnp.pad(
        a.reshape(4, heads, -1), ((0, 0), (0, GROUP - heads), (0, 0))
    ).reshape(4 * GROUP, -1)
    ours = lambda a: lax.dynamic_slice_in_dim(a, here * heads, heads, 1)
    gain = lax.dynamic_slice_in_dim(norm_gain, here * columns, columns, 1)
    steps_by_head = grouped(step_weight[0].T)
    shares = [
        call(
            functools.partial(partial_kernel, heads),
            f"partial_{e}",
            [((count, 2 * STATE + 4 * GROUP), BF16)],
        )(me, part, gain, state_weight[0], steps_by_head)[0]
        for e, part in enumerate(x)
    ]
    shares[1:] = [
        lax.ppermute(part, "ctx", [(i, i ^ d) for i in range(4)])
        for d, part in enumerate(shares[1:], 1)
    ]
    payloads = call(
        functools.partial(total_kernel, heads, width),
        "total",
        [((count + GROUP, 2 * STATE), BF16)] * 4,
        [pltpu.VMEM((4 * GROUP, 2 * count), BF16)],
    )(me, *shares, grouped(step_bias[0]).T)
    payloads[1:] = [
        lax.ppermute(part, "ctx", [(i, i ^ d) for i in range(4)])
        for d, part in enumerate(payloads[1:], 1)
    ]

    rate = jnp.tile(
        jnp.pad(-jnp.exp(ours(decay_log)), ((0, 0), (0, GROUP - heads))), (1, 4)
    )
    skip = jnp.repeat(ours(skip_gain), HEAD_DIM, axis=1)
    carry = carry_state[0].reshape(columns, STATE).T
    made = call(
        functools.partial(states_kernel, heads),
        "states",
        [
            ((count, 128), F32),
            ((128, count), F32),
            ((128, count), F32),
            ((4, STATE, columns), BF16),
        ],
        [pltpu.VMEM((4, STATE, columns), F32), pltpu.VMEM((4, 8, columns), F32)],
    )(me, *x, *payloads, gain, rate, carry)

    parts = [None] * 4
    for d in ORDER:
        [part] = call(functools.partial(output_kernel, heads, d), f"output_{d}", [block], flops=OUTPUT_FLOPS)(
            me, x[d], payloads[d], *made, gain, skip
        )
        route = [
            (s * 4 + c, ((s + 1) % sections) * 4 + (c ^ d))
            for s in range(sections)
            for c in range(4)
        ]
        parts[d] = lax.ppermute(part, ("section", "ctx"), route)
    [output] = call(
        join_kernel,
        "join",
        [((count, width), BF16)],
        [pltpu.SemaphoreType.DMA((4 * CUTS,))],
        where=pl.ANY,
        source=pl.ANY,
    )(me, *parts)
    return output[None]


def per_device(*arguments):
    activations, carry_state = arguments[0], arguments[-1]
    heads, dim, state = carry_state.shape[1:]
    fits = (
        lax.axis_size("ctx") == 4
        and activations.shape[1] == 128
        and (dim, state) == (HEAD_DIM, STATE)
        and heads % 2 == 0
        and heads < GROUP
    )
    return (by_heads if fits else by_positions)(*arguments)


def solution(mesh):
    placed = (
        P("section", "ctx", None),
        P("section", None),
        P("section", "ctx", None),
        P("section", "ctx", None),
        P("section", None),
        P("section", None),
        P("section", None),
        P("section", "ctx", None, None),
    )
    return jax.shard_map(
        per_device, mesh=mesh, in_specs=placed, out_specs=P("section", "ctx", None), check_vma=False
    )
```

```python
import functools
import math

import jax
import jax.numpy as jnp
from jax import lax
from jax.experimental import pallas as pl
from jax.experimental.pallas import tpu as pltpu
from jax.sharding import PartitionSpec as P

HEAD_DIM = 64
STATE = 128
EPS = 1e-05
GROUP = 32
VMEM_LIMIT = 24 << 20
CUTS = 4
ORDER = (3, 1, 2, 0)
EXCHANGES = (3, 1, 2)
SPLITS = ((3,), (1, 2), (0,))

F32, BF16 = jnp.float32, jnp.bfloat16


def entering(shard, axis, combine, identity):
    count, place = (lax.axis_size(axis), lax.axis_index(axis))
    everything = jax.tree.map(
        lambda part, kind: lax.all_gather(part.astype(kind), axis), shard, (BF16, BF16)
    )
    start = jax.tree.map(
        lambda part, zero: jnp.broadcast_to(jnp.asarray(zero, part.dtype), part.shape),
        shard,
        identity,
    )

    def lap(k, before):
        reached = k < place
        new = combine(
            before, jax.tree.map(lambda part, own: part[k].astype(own.dtype), everything, shard)
        )
        return jax.tree.map(lambda a, b: jnp.where(reached, a, b), new, before)

    return lax.fori_loop(0, count, lap, start)


def combine_states(earlier, later):
    return (earlier[0] + later[0], jnp.exp(later[0])[:, None, None] * earlier[1] + later[1])


def by_positions(
    activations, norm_gain, state_weight, step_weight, step_bias, decay_log, skip_gain, carry_state
):
    rows = activations[0]
    count = rows.shape[0]
    heads = step_weight.shape[2]
    inputs_f = rows.astype(F32)
    scale = lax.rsqrt(jnp.mean(inputs_f * inputs_f, axis=1, keepdims=True) + EPS)
    normed = (inputs_f * scale * norm_gain[0]).astype(BF16)
    first = jnp.dot(
        normed,
        lax.all_gather(state_weight, "ctx", axis=1, tiled=True)[0],
        preferred_element_type=F32,
    )
    second = jnp.dot(
        normed,
        lax.all_gather(step_weight, "ctx", axis=1, tiled=True)[0],
        preferred_element_type=F32,
    )
    b_rows = first[:, :STATE].astype(BF16)
    c_rows = first[:, STATE:].astype(BF16)
    step_size = jax.nn.softplus(second + step_bias[0])
    log_decay = -step_size * jnp.exp(decay_log[0])
    heads_x = normed.reshape(count, heads, HEAD_DIM)
    causal = jnp.arange(count)[:, None] >= jnp.arange(count)[None, :]
    cumulative = jnp.dot(causal.astype(F32), log_decay, precision=lax.Precision.HIGHEST)
    by_head = cumulative.T
    gap = by_head[:, :, None] - by_head[:, None, :]
    factor = jnp.where(causal[None], jnp.exp(jnp.where(causal[None], gap, 0.0)), 0.0)
    scores = jnp.dot(c_rows, b_rows.T, preferred_element_type=F32)
    mixing = (factor * scores[None] * step_size.T[:, None, :]).astype(BF16)
    intra = jnp.einsum("hts,shp->thp", mixing, heads_x, preferred_element_type=F32)
    tail = jnp.exp(cumulative[-1][None, :] - cumulative) * step_size
    weighted = (heads_x.astype(F32) * tail[:, :, None]).astype(BF16)
    block_state = jnp.einsum("shp,sn->hpn", weighted, b_rows, preferred_element_type=F32)
    carry_full = lax.all_gather(carry_state[0].astype(BF16), "ctx", axis=0, tiled=True).astype(F32)
    identity = (jnp.zeros((heads,), F32), jnp.zeros(block_state.shape, F32))
    prefix_decay, prefix_state = entering(
        (cumulative[-1], block_state), "ctx", combine_states, identity
    )
    start = jnp.exp(prefix_decay)[:, None, None] * carry_full + prefix_state
    inter = jnp.exp(cumulative)[:, :, None] * jnp.einsum(
        "tn,hpn->thp", c_rows, start.astype(BF16), preferred_element_type=F32
    )
    mixed = intra + inter + skip_gain[0][None, :, None] * heads_x.astype(F32)
    output = (inputs_f + mixed.reshape(count, heads * HEAD_DIM)).astype(BF16)
    sections = lax.axis_size("section")
    route = [(i, (i + 1) % sections) for i in range(sections)]
    return lax.ppermute(output[None], "section", route)


def params():
    return pltpu.CompilerParams(vmem_limit_bytes=VMEM_LIMIT)


def call(kernel, name, outs, scratch=(), where=pltpu.VMEM, source=pltpu.VMEM, flops=0):
    def run(me, *arrays):
        results = pl.pallas_call(
            kernel,
            out_shape=[jax.ShapeDtypeStruct(*o) for o in outs],
            in_specs=[pl.BlockSpec(memory_space=pltpu.SMEM)]
            + [pl.BlockSpec(memory_space=source)] * len(arrays),
            out_specs=[pl.BlockSpec(memory_space=where)] * len(outs),
            scratch_shapes=scratch,
            compiler_params=params(),
            cost_estimate=pl.CostEstimate(
                flops=flops,
                transcendentals=0,
                bytes_accessed=sum(a.size * a.dtype.itemsize for a in arrays)
                + sum(math.prod(shape) * jnp.dtype(kind).itemsize for shape, kind in outs),
            ),
            name=name,
        )(me, *arrays)
        return list(results)

    return run


def split_kernel(which, me_ref, x_ref, *refs):
    outs, sems = refs[-1 - len(which) : -1], refs[-1]
    count, columns = outs[0].shape
    me = me_ref[0]
    copies = []
    for i, (d, out) in enumerate(zip(which, outs)):
        at = pl.multiple_of(lax.bitwise_xor(me, d) * columns, 128)
        for k in range(CUTS):
            part = slice(k * count // CUTS, (k + 1) * count // CUTS)
            copies.append(
                pltpu.make_async_copy(
                    x_ref.at[part, pl.ds(at, columns)], out.at[part], sems.at[i * CUTS + k]
                )
            )
    for copy in copies:
        copy.start()
    for copy in copies:
        copy.wait()


def join_kernel(me_ref, *refs):
    parts, out, sems = refs[:-2], refs[-2], refs[-1]
    count, columns = parts[0].shape
    me = me_ref[0]
    copies = []
    for d, block in enumerate(parts):
        at = pl.multiple_of(lax.bitwise_xor(me, d) * columns, 128)
        for k in range(CUTS):
            part = slice(k * count // CUTS, (k + 1) * count // CUTS)
            copies.append(
                pltpu.make_async_copy(
                    block.at[part], out.at[part, pl.ds(at, columns)], sems.at[d * CUTS + k]
                )
            )
    for copy in copies:
        copy.start()
    for copy in copies:
        copy.wait()


def lanes_of(shape):
    return lax.broadcasted_iota(jnp.int32, shape, 1)


def partial_kernel(heads, _, x_ref, gain_ref, w_ref, ws_ref, out_ref):
    x = x_ref[...].astype(F32)
    squares = jnp.sum(x * x, axis=1, keepdims=True)
    high = squares.astype(BF16).astype(F32)
    scaled = (x * gain_ref[...]).astype(BF16)
    rows = jnp.dot(scaled, w_ref[...], preferred_element_type=F32)
    raw = lax.dot_general(scaled, ws_ref[...], (((1,), (1,)), ((), ())), preferred_element_type=F32)
    lane = lanes_of(raw.shape)
    raw = jnp.where(lane == heads, high, raw)
    raw = jnp.where(lane == heads + 1, squares - high, raw)
    out_ref[:, : 2 * STATE] = rows.astype(BF16)
    out_ref[:, 2 * STATE :] = raw.astype(BF16)


def total_kernel(
    heads, width, me_ref, p0, p1, p2, p3, bias_ref, o0, o1, o2, o3, turned
):
    count = p0.shape[0]
    me = me_ref[0]
    total = sum(p[...].astype(F32) for p in (p0, p1, p2, p3))
    rows, raw = total[:, : 2 * STATE], total[:, 2 * STATE :]
    lane = lanes_of(raw.shape)
    squares = raw[:, heads : heads + 1] + raw[:, heads + 1 : heads + 2]
    scale = lax.rsqrt(jnp.broadcast_to(squares, raw.shape) * (1.0 / width) + EPS)
    biased = raw * scale + bias_ref[...]
    step = jnp.maximum(biased, 0.0) + jnp.log1p(jnp.exp(-jnp.abs(biased)))
    step = jnp.where(lane % GROUP == heads, scale, step)
    step = jnp.where(lane % GROUP > heads, 0.0, step)
    by_head = step.T
    high = by_head.astype(BF16)
    turned[:, :count] = high
    turned[:, count:] = (by_head - high.astype(F32)).astype(BF16)
    both = jnp.concatenate(
        [(rows[:, :STATE] * scale).T, rows[:, STATE:] * scale], axis=1
    ).astype(BF16)
    for d, out in enumerate((o0, o1, o2, o3)):
        at = pl.multiple_of(lax.bitwise_xor(me, d) * GROUP, GROUP)
        out[:count, :] = both
        out[count:, :] = turned[pl.ds(at, GROUP), :]


def pieces(values, e, lane):
    values = pltpu.roll(values, -e * GROUP % 128, 1) if e else values
    high = values.astype(BF16).astype(F32)
    low = pltpu.roll(values - high, GROUP, 1)
    return jnp.where(lane < GROUP, high, jnp.where(lane < 2 * GROUP, low, 0.0)).astype(BF16)


def states_kernel(
    heads, me_ref, x0, x1, x2, x3, p0, p1, p2, p3, gain_ref, rate_ref, carry_ref,
    spread_ref, cum_ref, cumt_ref, stept_ref, start_ref, made, kept,
):
    count, columns = x0.shape
    me = me_ref[0]
    lane = lanes_of((count, 128))
    payloads = (p0, p1, p2, p3)
    by_head = jnp.concatenate(
        [p[count:, :count].astype(F32) + p[count:, count:].astype(F32) for p in payloads]
    )
    stept_ref[...] = by_head
    step = by_head.T
    log_decay = step * rate_ref[...]
    lower = lax.broadcasted_iota(jnp.int32, (count, count), 0) >= lax.broadcasted_iota(
        jnp.int32, (count, count), 1
    )
    cum = jnp.dot(
        lower.astype(F32),
        log_decay,
        precision=lax.Precision.HIGHEST,
        preferred_element_type=F32,
    )
    last = cum[count - 1 : count, :]
    tail = jnp.exp(last - cum) * step
    decay = jnp.exp(last)
    cum_ref[...] = jnp.where(lane % GROUP == heads, step, cum)
    cumt_ref[...] = cum.T
    scales = [
        jnp.broadcast_to(step[:, at : at + 1], (count, 128))
        for at in range(heads, 4 * GROUP, GROUP)
    ]
    decays = jnp.broadcast_to(decay, (8, 128))
    terms = jnp.concatenate(
        [pieces(tail, e, lane) for e in range(4)] + [pieces(decays, e, lane[:8]) for e in range(4)]
    )
    for j in range(0, columns, 256):
        wide = jnp.dot(terms, spread_ref[:, j : j + 256], preferred_element_type=F32)
        for e, x_ref in enumerate((x0, x1, x2, x3)):
            block = lax.bitwise_xor(me, e)
            x = x_ref[:, j : j + 256].astype(F32)
            scale = jnp.concatenate([scales[e]] * 2, axis=1)
            normed = (x * scale * gain_ref[:, j : j + 256]).astype(BF16).astype(F32)
            weighted = (normed * wide[e * count : (e + 1) * count]).astype(BF16)
            kept[block, :, j : j + 256] = wide[4 * count + 8 * e : 4 * count + 8 * (e + 1)]
            made[block, :, j : j + 256] = jnp.dot(
                payloads[e][:count, :STATE], weighted, preferred_element_type=F32
            )
    for j in range(columns // 128):
        at = slice(j * 128, (j + 1) * 128)
        state = carry_ref[:, at]
        for t in range(4):
            start_ref[lax.bitwise_xor(me, t), :, at] = state.astype(BF16)
            if t < 3:
                state = kept[t, 0:1, at] * state + made[t, :, at]


def output_kernel(
    heads, e, _, x_ref, payload_ref, cum_ref, cumt_ref, stept_ref, start_ref, gain_ref, skip_ref,
    spread_ref, out_ref,
):
    count, columns = x_ref.shape
    lane = lanes_of((count, 128))
    b_turned, c_rows = payload_ref[:count, :STATE], payload_ref[:count, STATE:]
    cum = cum_ref[...]
    grown = jnp.dot(pieces(jnp.exp(cum), e, lane), spread_ref[...], preferred_element_type=F32)
    at = e * GROUP + heads
    scale = jnp.broadcast_to(cum[:, at : at + 1], (count, 128))
    lower = lax.broadcasted_iota(jnp.int32, (count, count), 0) >= lax.broadcasted_iota(
        jnp.int32, (count, count), 1
    )
    scores = jnp.dot(c_rows, b_turned, preferred_element_type=F32)
    scores = jnp.where(lower, scores, 0.0)
    for j in range(columns // 128):
        at = slice(j * 128, (j + 1) * 128)
        x = x_ref[:, at].astype(F32)
        low = (x * scale * gain_ref[:, at]).astype(BF16)
        normed = low.astype(F32)
        mixing, spread = [], []
        for k in range(2):
            column = e * GROUP + 2 * j + k
            row = column
            gap = cum[:, column : column + 1] - cumt_ref[row : row + 1, :]
            factor = jnp.exp(jnp.where(lower, gap, 0.0))
            mixing.append((factor * scores * stept_ref[row : row + 1, :]).astype(BF16))
            mine = (lane < HEAD_DIM) if k == 0 else (lane >= HEAD_DIM)
            spread.append(jnp.where(mine, normed, 0.0).astype(BF16))
        intra = jnp.dot(
            jnp.concatenate(mixing, axis=1),
            jnp.concatenate(spread, axis=0),
            preferred_element_type=F32,
        )
        inter = jnp.dot(c_rows, start_ref[e, :, at], preferred_element_type=F32)
        mixed = intra + grown[:, at] * inter + skip_ref[:, at] * normed
        out_ref[:, at] = (x + mixed).astype(BF16)


def first_kernel(
    heads, e, me_ref, x0, x1, x2, x3, p0, p1, p2, p3, gain_ref, rate_ref, carry_ref, skip_ref,
    spread_ref, cum_ref, cumt_ref, stept_ref, start_ref, out_ref, made, kept,
):
    x, payloads = (x0, x1, x2, x3), (p0, p1, p2, p3)
    states_kernel(
        heads, me_ref, *x, *payloads, gain_ref, rate_ref, carry_ref,
        spread_ref, cum_ref, cumt_ref, stept_ref, start_ref, made, kept,
    )
    output_kernel(
        heads, e, me_ref, x[e], payloads[e], cum_ref, cumt_ref, stept_ref, start_ref, gain_ref,
        skip_ref, spread_ref, out_ref,
    )


def by_heads(
    activations, norm_gain, state_weight, step_weight, step_bias, decay_log, skip_gain, carry_state
):
    rows = activations[0]
    count, width = rows.shape
    heads = carry_state.shape[1]
    columns = heads * HEAD_DIM
    here = lax.axis_index("ctx")
    me = here.astype(jnp.int32).reshape(1)
    sections = lax.axis_size("section")
    block = ((count, columns), BF16)

    x = [None] * 4
    source = pltpu.with_memory_space_constraint(rows, pltpu.HBM)
    before = []
    for which in SPLITS:
        made = call(
            functools.partial(split_kernel, which),
            "split_" + "".join(map(str, which)),
            [block] * len(which),
            [pltpu.SemaphoreType.DMA((len(which) * CUTS,))],
            source=pl.ANY,
        )(me, source, *before)
        for d, part in zip(which, made):
            x[d] = part
        before = made[:1]
    for d in EXCHANGES:
        x[d] = lax.ppermute(x[d], "ctx", [(i, i ^ d) for i in range(4)])

    grouped = lambda a: jnp.pad(
        a.reshape(4, heads, -1), ((0, 0), (0, GROUP - heads), (0, 0))
    ).reshape(4 * GROUP, -1)
    ours = lambda a: lax.dynamic_slice_in_dim(a, here * heads, heads, 1)
    gain = lax.dynamic_slice_in_dim(norm_gain, here * columns, columns, 1)
    steps_by_head = grouped(step_weight[0].T)
    shares = [None] * 4
    for d in (0, *EXCHANGES):
        [shares[d]] = call(
            functools.partial(partial_kernel, heads),
            f"partial_{d}",
            [((count, 2 * STATE + 4 * GROUP), BF16)],
        )(me, x[d], gain, state_weight[0], steps_by_head)
        if d:
            shares[d] = lax.ppermute(shares[d], "ctx", [(i, i ^ d) for i in range(4)])
    payloads = call(
        functools.partial(total_kernel, heads, width),
        "total",
        [((count + GROUP, 2 * STATE), BF16)] * 4,
        [pltpu.VMEM((4 * GROUP, 2 * count), BF16)],
    )(me, *shares, grouped(step_bias[0]).T)
    for d in EXCHANGES:
        payloads[d] = lax.ppermute(payloads[d], "ctx", [(i, i ^ d) for i in range(4)])

    rate = jnp.tile(
        jnp.pad(-jnp.exp(ours(decay_log)), ((0, 0), (0, GROUP - heads))), (1, 4)
    )
    skip = jnp.repeat(ours(skip_gain), HEAD_DIM, axis=1)
    carry = carry_state[0].reshape(columns, STATE).T
    row = lax.broadcasted_iota(jnp.int32, (128, columns), 0)
    head = lax.broadcasted_iota(jnp.int32, (128, columns), 1) // HEAD_DIM
    spread = ((row % GROUP == head) & (row < 2 * GROUP)).astype(BF16)
    *made, first = call(
        functools.partial(first_kernel, heads, ORDER[0]),
        "first",
        [
            ((count, 128), F32),
            ((128, count), F32),
            ((128, count), F32),
            ((4, STATE, columns), BF16),
            block,
        ],
        [pltpu.VMEM((4, STATE, columns), F32), pltpu.VMEM((4, 8, columns), F32)],
    )(me, *x, *payloads, gain, rate, carry, skip, spread)

    parts = [None] * 4
    for d in ORDER:
        part = first
        if d != ORDER[0]:
            [part] = call(functools.partial(output_kernel, heads, d), f"output_{d}", [block])(
                me, x[d], payloads[d], *made, gain, skip, spread
            )
        route = [
            (s * 4 + c, ((s + 1) % sections) * 4 + (c ^ d))
            for s in range(sections)
            for c in range(4)
        ]
        parts[d] = lax.ppermute(part, ("section", "ctx"), route)
    [output] = call(
        join_kernel,
        "join",
        [((count, width), BF16)],
        [pltpu.SemaphoreType.DMA((4 * CUTS,))],
        where=pl.ANY,
        source=pl.ANY,
    )(me, *parts)
    return output[None]


def per_device(*arguments):
    activations, carry_state = arguments[0], arguments[-1]
    heads, dim, state = carry_state.shape[1:]
    fits = (
        lax.axis_size("ctx") == 4
        and activations.shape[1] == 128
        and (dim, state) == (HEAD_DIM, STATE)
        and heads % 2 == 0
        and heads < GROUP
    )
    return (by_heads if fits else by_positions)(*arguments)


def solution(mesh):
    placed = (
        P("section", "ctx", None),
        P("section", None),
        P("section", "ctx", None),
        P("section", "ctx", None),
        P("section", None),
        P("section", None),
        P("section", None),
        P("section", "ctx", None, None),
    )
    return jax.shard_map(
        per_device, mesh=mesh, in_specs=placed, out_specs=P("section", "ctx", None), check_vma=False
    )
```

```python
import functools
import math

import jax
import jax.numpy as jnp
from jax import lax
from jax.experimental import pallas as pl
from jax.experimental.pallas import tpu as pltpu
from jax.sharding import PartitionSpec as P

HEAD_DIM = 64
STATE = 128
EPS = 1e-05
GROUP = 32
VMEM_LIMIT = 24 << 20
CUTS = 4
ORDER = (3, 1, 2, 0)
EXCHANGES = (3, 1, 2)
JOINS = ((3, 1, 2), (0,))
SPLITS = ((3,), (1, 2), (0,))

F32, BF16 = jnp.float32, jnp.bfloat16


def entering(shard, axis, combine, identity):
    count, place = (lax.axis_size(axis), lax.axis_index(axis))
    everything = jax.tree.map(
        lambda part, kind: lax.all_gather(part.astype(kind), axis), shard, (BF16, BF16)
    )
    start = jax.tree.map(
        lambda part, zero: jnp.broadcast_to(jnp.asarray(zero, part.dtype), part.shape),
        shard,
        identity,
    )

    def lap(k, before):
        reached = k < place
        new = combine(
            before, jax.tree.map(lambda part, own: part[k].astype(own.dtype), everything, shard)
        )
        return jax.tree.map(lambda a, b: jnp.where(reached, a, b), new, before)

    return lax.fori_loop(0, count, lap, start)


def combine_states(earlier, later):
    return (earlier[0] + later[0], jnp.exp(later[0])[:, None, None] * earlier[1] + later[1])


def by_positions(
    activations, norm_gain, state_weight, step_weight, step_bias, decay_log, skip_gain, carry_state
):
    rows = activations[0]
    count = rows.shape[0]
    heads = step_weight.shape[2]
    inputs_f = rows.astype(F32)
    scale = lax.rsqrt(jnp.mean(inputs_f * inputs_f, axis=1, keepdims=True) + EPS)
    normed = (inputs_f * scale * norm_gain[0]).astype(BF16)
    first = jnp.dot(
        normed,
        lax.all_gather(state_weight, "ctx", axis=1, tiled=True)[0],
        preferred_element_type=F32,
    )
    second = jnp.dot(
        normed,
        lax.all_gather(step_weight, "ctx", axis=1, tiled=True)[0],
        preferred_element_type=F32,
    )
    b_rows = first[:, :STATE].astype(BF16)
    c_rows = first[:, STATE:].astype(BF16)
    step_size = jax.nn.softplus(second + step_bias[0])
    log_decay = -step_size * jnp.exp(decay_log[0])
    heads_x = normed.reshape(count, heads, HEAD_DIM)
    causal = jnp.arange(count)[:, None] >= jnp.arange(count)[None, :]
    cumulative = jnp.dot(causal.astype(F32), log_decay, precision=lax.Precision.HIGHEST)
    by_head = cumulative.T
    gap = by_head[:, :, None] - by_head[:, None, :]
    factor = jnp.where(causal[None], jnp.exp(jnp.where(causal[None], gap, 0.0)), 0.0)
    scores = jnp.dot(c_rows, b_rows.T, preferred_element_type=F32)
    mixing = (factor * scores[None] * step_size.T[:, None, :]).astype(BF16)
    intra = jnp.einsum("hts,shp->thp", mixing, heads_x, preferred_element_type=F32)
    tail = jnp.exp(cumulative[-1][None, :] - cumulative) * step_size
    weighted = (heads_x.astype(F32) * tail[:, :, None]).astype(BF16)
    block_state = jnp.einsum("shp,sn->hpn", weighted, b_rows, preferred_element_type=F32)
    carry_full = lax.all_gather(carry_state[0].astype(BF16), "ctx", axis=0, tiled=True).astype(F32)
    identity = (jnp.zeros((heads,), F32), jnp.zeros(block_state.shape, F32))
    prefix_decay, prefix_state = entering(
        (cumulative[-1], block_state), "ctx", combine_states, identity
    )
    start = jnp.exp(prefix_decay)[:, None, None] * carry_full + prefix_state
    inter = jnp.exp(cumulative)[:, :, None] * jnp.einsum(
        "tn,hpn->thp", c_rows, start.astype(BF16), preferred_element_type=F32
    )
    mixed = intra + inter + skip_gain[0][None, :, None] * heads_x.astype(F32)
    output = (inputs_f + mixed.reshape(count, heads * HEAD_DIM)).astype(BF16)
    sections = lax.axis_size("section")
    route = [(i, (i + 1) % sections) for i in range(sections)]
    return lax.ppermute(output[None], "section", route)


def params():
    return pltpu.CompilerParams(vmem_limit_bytes=VMEM_LIMIT)


def call(kernel, name, outs, scratch=(), where=pltpu.VMEM, source=pltpu.VMEM, flops=0, aliases={}):
    def run(me, *arrays):
        results = pl.pallas_call(
            kernel,
            out_shape=[jax.ShapeDtypeStruct(*o) for o in outs],
            in_specs=[pl.BlockSpec(memory_space=pltpu.SMEM)]
            + [pl.BlockSpec(memory_space=source)] * len(arrays),
            out_specs=[pl.BlockSpec(memory_space=where)] * len(outs),
            scratch_shapes=scratch,
            compiler_params=params(),
            input_output_aliases=aliases,
            cost_estimate=pl.CostEstimate(
                flops=flops,
                transcendentals=0,
                bytes_accessed=sum(a.size * a.dtype.itemsize for a in arrays)
                + sum(math.prod(shape) * jnp.dtype(kind).itemsize for shape, kind in outs),
            ),
            name=name,
        )(me, *arrays)
        return list(results)

    return run


def split_kernel(which, me_ref, x_ref, *refs):
    outs, sems = refs[-1 - len(which) : -1], refs[-1]
    count, columns = outs[0].shape
    me = me_ref[0]
    copies = []
    for i, (d, out) in enumerate(zip(which, outs)):
        at = pl.multiple_of(lax.bitwise_xor(me, d) * columns, 128)
        for k in range(CUTS):
            part = slice(k * count // CUTS, (k + 1) * count // CUTS)
            copies.append(
                pltpu.make_async_copy(
                    x_ref.at[part, pl.ds(at, columns)], out.at[part], sems.at[i * CUTS + k]
                )
            )
    for copy in copies:
        copy.start()
    for copy in copies:
        copy.wait()


def join_kernel(which, me_ref, *refs):
    parts, out, sems = refs[: len(which)], refs[-2], refs[-1]
    count, columns = parts[0].shape
    me = me_ref[0]
    copies = []
    for i, (d, block) in enumerate(zip(which, parts)):
        at = pl.multiple_of(lax.bitwise_xor(me, d) * columns, 128)
        for k in range(CUTS):
            part = slice(k * count // CUTS, (k + 1) * count // CUTS)
            copies.append(
                pltpu.make_async_copy(
                    block.at[part], out.at[part, pl.ds(at, columns)], sems.at[i * CUTS + k]
                )
            )
    for copy in copies:
        copy.start()
    for copy in copies:
        copy.wait()


def lanes_of(shape):
    return lax.broadcasted_iota(jnp.int32, shape, 1)


def partial_kernel(heads, _, x_ref, gain_ref, w_ref, ws_ref, out_ref):
    x = x_ref[...].astype(F32)
    squares = jnp.sum(x * x, axis=1, keepdims=True)
    high = squares.astype(BF16).astype(F32)
    scaled = (x * gain_ref[...]).astype(BF16)
    rows = jnp.dot(scaled, w_ref[...], preferred_element_type=F32)
    raw = lax.dot_general(scaled, ws_ref[...], (((1,), (1,)), ((), ())), preferred_element_type=F32)
    lane = lanes_of(raw.shape)
    raw = jnp.where(lane == heads, high, raw)
    raw = jnp.where(lane == heads + 1, squares - high, raw)
    out_ref[:, : 2 * STATE] = rows.astype(BF16)
    out_ref[:, 2 * STATE :] = raw.astype(BF16)


def total_kernel(
    heads, width, me_ref, p0, p1, p2, p3, bias_ref, o3, keep, turned
):
    count = p0.shape[0]
    me = me_ref[0]
    total = sum(p[...].astype(F32) for p in (p0, p1, p2, p3))
    rows, raw = total[:, : 2 * STATE], total[:, 2 * STATE :]
    lane = lanes_of(raw.shape)
    squares = raw[:, heads : heads + 1] + raw[:, heads + 1 : heads + 2]
    scale = lax.rsqrt(jnp.broadcast_to(squares, raw.shape) * (1.0 / width) + EPS)
    biased = raw * scale + bias_ref[...]
    step = jnp.maximum(biased, 0.0) + jnp.log1p(jnp.exp(-jnp.abs(biased)))
    step = jnp.where(lane % GROUP == heads, scale, step)
    step = jnp.where(lane % GROUP > heads, 0.0, step)
    by_head = step.T
    high = by_head.astype(BF16)
    turned[:, :count] = high
    turned[:, count:] = (by_head - high.astype(F32)).astype(BF16)
    both = jnp.concatenate(
        [(rows[:, :STATE] * scale).T, rows[:, STATE:] * scale], axis=1
    ).astype(BF16)
    for d, out in ((3, o3), (0, keep)):
        put(me, d, both, turned, out)


def put(me, d, both, turned, out):
    count = both.shape[0]
    at = pl.multiple_of(lax.bitwise_xor(me, d) * GROUP, GROUP)
    out[:count, :] = both
    out[count:, :] = turned[pl.ds(at, GROUP), :]


def rest_kernel(me_ref, keep_ref, turned_ref, o1, o2):
    for d, out in ((1, o1), (2, o2)):
        put(me_ref[0], d, keep_ref[: keep_ref.shape[0] - GROUP, :], turned_ref, out)


def pieces(values, e, lane):
    values = pltpu.roll(values, -e * GROUP % 128, 1) if e else values
    high = values.astype(BF16).astype(F32)
    low = pltpu.roll(values - high, GROUP, 1)
    return jnp.where(lane < GROUP, high, jnp.where(lane < 2 * GROUP, low, 0.0)).astype(BF16)


def decays_of(heads, payloads, rate_ref, cum_ref, cumt_ref, stept_ref):
    count = cum_ref.shape[0]
    lane = lanes_of((count, 128))
    rows = [p[count:, :count].astype(F32) + p[count:, count:].astype(F32) for p in payloads]
    rest = [jnp.zeros((128 - 2 * GROUP, count), F32)]
    step = jnp.concatenate(rows + rest).T
    by_head = jnp.concatenate([r * r[heads : heads + 1, :] for r in rows] + rest)
    stept_ref[...] = by_head
    cum = jnp.dot(
        lower_half(count).astype(F32),
        step * rate_ref[...],
        precision=lax.Precision.HIGHEST,
        preferred_element_type=F32,
    )
    cum_ref[...] = jnp.where(lane % GROUP == heads, step, cum)
    cumt_ref[...] = cum.T
    last = cum[count - 1 : count, :]
    return jnp.exp(last - cum) * by_head.T, jnp.exp(last)


def lower_half(count):
    return lax.broadcasted_iota(jnp.int32, (count, count), 0) >= lax.broadcasted_iota(
        jnp.int32, (count, count), 1
    )


def block_states(x, payloads, tail, decay, spread_ref, made, kept):
    count, columns = x[0].shape
    lane = lanes_of((count, 128))
    decays = jnp.broadcast_to(decay, (8, 128))
    terms = jnp.concatenate(
        [pieces(tail, i, lane) for i in range(2)] + [pieces(decays, i, lane[:8]) for i in range(2)]
    )
    for j in range(0, columns, 256):
        at = slice(j, j + 256)
        wide = jnp.dot(terms, spread_ref[:, at], preferred_element_type=F32)
        for i in range(2):
            weighted = x[i][:, at].astype(F32) * wide[i * count : (i + 1) * count]
            kept[i][:, at] = wide[2 * count + 8 * i : 2 * count + 8 * (i + 1)]
            made[i][:, at] = jnp.dot(
                payloads[i][:count, :STATE], weighted.astype(BF16), preferred_element_type=F32
            )


def within_block(heads, i, x_ref, payload_ref, cum_ref, cumt_ref, stept_ref, gain_ref, skip_ref):
    count, columns = x_ref.shape
    lane = lanes_of((count, 128))
    cum = cum_ref[...]
    at = i * GROUP + heads
    scale = jnp.broadcast_to(cum[:, at : at + 1], (count, 128))
    lower = lower_half(count)
    scores = jnp.dot(
        payload_ref[:count, STATE:], payload_ref[:count, :STATE], preferred_element_type=F32
    )
    scores = jnp.where(lower, scores, 0.0)
    for j in range(columns // 128):
        at = slice(j * 128, (j + 1) * 128)
        low = x_ref[:, at]
        x = low.astype(F32)
        mixing, spread = [], []
        for k in range(2):
            row = i * GROUP + 2 * j + k
            gap = cum[:, row : row + 1] - cumt_ref[row : row + 1, :]
            factor = jnp.exp(jnp.where(lower, gap, 0.0))
            mixing.append((factor * scores * stept_ref[row : row + 1, :]).astype(BF16))
            mine = (lane < HEAD_DIM) if k == 0 else (lane >= HEAD_DIM)
            spread.append(jnp.where(mine, low, jnp.zeros_like(low)))
        intra = jnp.dot(
            jnp.concatenate(mixing, axis=1),
            jnp.concatenate(spread, axis=0),
            preferred_element_type=F32,
        )
        gain = gain_ref[:, at]
        yield at, x + (gain * intra + (skip_ref[:, at] * gain) * (x * scale))


def output_kernel(
    heads, e, i, _, x_ref, payload_ref, cum_ref, cumt_ref, stept_ref, start_ref, gain_ref, skip_ref,
    spread_ref, out_ref,
):
    count = x_ref.shape[0]
    grown = jnp.exp(cum_ref[...])
    grown = jnp.dot(
        pieces(grown, i, lanes_of(grown.shape)), spread_ref[...], preferred_element_type=F32
    )
    for at, inside in within_block(
        heads, i, x_ref, payload_ref, cum_ref, cumt_ref, stept_ref, gain_ref, skip_ref
    ):
        inter = jnp.dot(
            payload_ref[:count, STATE:], start_ref[e, :, at], preferred_element_type=F32
        )
        out_ref[:, at] = (inside + grown[:, at] * inter).astype(BF16)


def early_kernel(
    heads, _, x0, x3, p0, p3, gain_ref, rate_ref, skip_ref, spread_ref,
    cum_ref, cumt_ref, stept_ref, m0, m3, k0, k3, inside_ref, grown_ref,
):
    tail, decay = decays_of(heads, (p0, p3), rate_ref, cum_ref, cumt_ref, stept_ref)
    block_states((x0, x3), (p0, p3), tail, decay, spread_ref, (m0, m3), (k0, k3))
    grown = jnp.exp(cum_ref[...])
    grown_ref[...] = jnp.dot(
        pieces(grown, 1, lanes_of(grown.shape)), spread_ref[...], preferred_element_type=F32
    )
    for at, inside in within_block(
        heads, 1, x3, p3, cum_ref, cumt_ref, stept_ref, gain_ref, skip_ref
    ):
        inside_ref[:, at] = inside


def first_kernel(
    heads, me_ref, x1, x2, p1, p2, p3, m0, m3, k0, k3, inside_ref, grown_ref, gain_ref, rate_ref,
    carry_ref, spread_ref, cum_ref, cumt_ref, stept_ref, start_ref, out_ref, m1, m2, k1, k2,
):
    count, columns = x1.shape
    tail, decay = decays_of(heads, (p1, p2), rate_ref, cum_ref, cumt_ref, stept_ref)
    block_states((x1, x2), (p1, p2), tail, decay, spread_ref, (m1, m2), (k1, k2))
    made, kept = (m0, m1, m2, m3), (k0, k1, k2, k3)

    def follow(me):
        for j in range(columns // 128):
            at = slice(j * 128, (j + 1) * 128)
            state = carry_ref[:, at]
            for t in range(4):
                start_ref[t ^ me, :, at] = state.astype(BF16)
                if t < 3:
                    state = kept[t ^ me][0:1, at] * state + gain_ref[:, at] * made[t ^ me][:, at]

    for me in range(4):
        pl.when(me_ref[0] == me)(functools.partial(follow, me))
    for j in range(0, columns, 256):
        at = slice(j, j + 256)
        inter = jnp.dot(p3[:count, STATE:], start_ref[3, :, at], preferred_element_type=F32)
        out_ref[:, at] = (inside_ref[:, at] + grown_ref[:, at] * inter).astype(BF16)


def by_heads(
    activations, norm_gain, state_weight, step_weight, step_bias, decay_log, skip_gain, carry_state
):
    rows = activations[0]
    count, width = rows.shape
    heads = carry_state.shape[1]
    columns = heads * HEAD_DIM
    here = lax.axis_index("ctx")
    me = here.astype(jnp.int32).reshape(1)
    sections = lax.axis_size("section")
    block = ((count, columns), BF16)

    x = [None] * 4
    source = pltpu.with_memory_space_constraint(rows, pltpu.HBM)
    before = []
    for which in SPLITS:
        made = call(
            functools.partial(split_kernel, which),
            "split_" + "".join(map(str, which)),
            [block] * len(which),
            [pltpu.SemaphoreType.DMA((len(which) * CUTS,))],
            source=pl.ANY,
        )(me, source, *before)
        for d, part in zip(which, made):
            x[d] = part
        before = made[:1]
    for d in EXCHANGES:
        x[d] = lax.ppermute(x[d], "ctx", [(i, i ^ d) for i in range(4)])

    grouped = lambda a: jnp.pad(
        a.reshape(4, heads, -1), ((0, 0), (0, GROUP - heads), (0, 0))
    ).reshape(4 * GROUP, -1)
    ours = lambda a: lax.dynamic_slice_in_dim(a, here * heads, heads, 1)
    gain = lax.dynamic_slice_in_dim(norm_gain, here * columns, columns, 1)
    steps_by_head = grouped(step_weight[0].T)
    shares = [None] * 4
    for d in (0, *EXCHANGES):
        [shares[d]] = call(
            functools.partial(partial_kernel, heads),
            f"partial_{d}",
            [((count, 2 * STATE + 4 * GROUP), BF16)],
        )(me, x[d], gain, state_weight[0], steps_by_head)
        if d:
            shares[d] = lax.ppermute(shares[d], "ctx", [(i, i ^ d) for i in range(4)])
    payload = ((count + GROUP, 2 * STATE), BF16)
    payloads = [None] * 4
    payloads[3], payloads[0], turned = call(
        functools.partial(total_kernel, heads, width),
        "total",
        [payload, payload, ((4 * GROUP, 2 * count), BF16)],
    )(me, *shares, grouped(step_bias[0]).T)
    payloads[1:3] = call(rest_kernel, "rest", [payload] * 2)(me, payloads[0], turned)
    for d in EXCHANGES:
        payloads[d] = lax.ppermute(payloads[d], "ctx", [(i, i ^ d) for i in range(4)])

    rate = jnp.tile(
        jnp.pad(-jnp.exp(ours(decay_log)), ((0, 0), (0, GROUP - heads))), (1, 4)
    )
    skip = jnp.repeat(ours(skip_gain), HEAD_DIM, axis=1)
    carry = carry_state[0].reshape(columns, STATE).T
    row = lax.broadcasted_iota(jnp.int32, (128, columns), 0)
    head = lax.broadcasted_iota(jnp.int32, (128, columns), 1) // HEAD_DIM
    spread = ((row % GROUP == head) & (row < 2 * GROUP)).astype(BF16)
    decays = [((count, 128), F32), ((128, count), F32), ((128, count), F32)]
    state, left, whole = ((STATE, columns), F32), ((8, columns), F32), ((count, columns), F32)
    *early, m0, m3, k0, k3, inside, grown = call(
        functools.partial(early_kernel, heads),
        "early",
        [*decays, state, state, left, left, whole, whole],
    )(me, x[0], x[3], payloads[0], payloads[3], gain, rate, skip, spread)
    *late, start, first = call(
        functools.partial(first_kernel, heads),
        "first",
        [*decays, ((4, STATE, columns), BF16), block],
        [pltpu.VMEM(*shape) for shape in (state, state, left, left)],
    )(me, *x[1:3], *payloads[1:], m0, m3, k0, k3, inside, grown, gain, rate, carry, spread)
    timed = {0: (0, early), 1: (0, late), 2: (1, late)}

    parts = [None] * 4
    for d in ORDER:
        part = first
        if d != ORDER[0]:
            i, made = timed[d]
            [part] = call(
                functools.partial(output_kernel, heads, d, i), f"output_{d}", [block]
            )(me, x[d], payloads[d], *made, start, gain, skip, spread)
        route = [
            (s * 4 + c, ((s + 1) % sections) * 4 + (c ^ d))
            for s in range(sections)
            for c in range(4)
        ]
        parts[d] = lax.ppermute(part, ("section", "ctx"), route)
    output = []
    for which in JOINS:
        output = call(
            functools.partial(join_kernel, which),
            "join_" + "".join(map(str, which)),
            [((count, width), BF16)],
            [pltpu.SemaphoreType.DMA((len(which) * CUTS,))],
            where=pl.ANY,
            source=pl.ANY,
            aliases={1 + len(which): 0} if output else {},
        )(me, *[parts[d] for d in which], *output)
    return output[0][None]


def per_device(*arguments):
    activations, carry_state = arguments[0], arguments[-1]
    heads, dim, state = carry_state.shape[1:]
    fits = (
        lax.axis_size("ctx") == 4
        and activations.shape[1] == 128
        and (dim, state) == (HEAD_DIM, STATE)
        and heads % 2 == 0
        and heads < GROUP
    )
    return (by_heads if fits else by_positions)(*arguments)


def solution(mesh):
    placed = (
        P("section", "ctx", None),
        P("section", None),
        P("section", "ctx", None),
        P("section", "ctx", None),
        P("section", None),
        P("section", None),
        P("section", None),
        P("section", "ctx", None, None),
    )
    return jax.shard_map(
        per_device, mesh=mesh, in_specs=placed, out_specs=P("section", "ctx", None), check_vma=False
    )
```

```python
import functools
import math

import jax
import jax.numpy as jnp
from jax import lax
from jax.experimental import pallas as pl
from jax.experimental.pallas import tpu as pltpu
from jax.sharding import PartitionSpec as P

HEAD_DIM = 64
STATE = 128
EPS = 1e-05
GROUP = 32
VMEM_LIMIT = 24 << 20
CUTS = 4
ORDER = (3, 1, 2, 0)
EXCHANGES = (3, 1, 2)
JOINS = ((3, 1, 2), (0,))
SPLITS = ((3,), (2, 1), (0,))

F32, BF16 = jnp.float32, jnp.bfloat16


def entering(shard, axis, combine, identity):
    count, place = (lax.axis_size(axis), lax.axis_index(axis))
    everything = jax.tree.map(
        lambda part, kind: lax.all_gather(part.astype(kind), axis), shard, (BF16, BF16)
    )
    start = jax.tree.map(
        lambda part, zero: jnp.broadcast_to(jnp.asarray(zero, part.dtype), part.shape),
        shard,
        identity,
    )

    def lap(k, before):
        reached = k < place
        new = combine(
            before, jax.tree.map(lambda part, own: part[k].astype(own.dtype), everything, shard)
        )
        return jax.tree.map(lambda a, b: jnp.where(reached, a, b), new, before)

    return lax.fori_loop(0, count, lap, start)


def combine_states(earlier, later):
    return (earlier[0] + later[0], jnp.exp(later[0])[:, None, None] * earlier[1] + later[1])


def by_positions(
    activations, norm_gain, state_weight, step_weight, step_bias, decay_log, skip_gain, carry_state
):
    rows = activations[0]
    count = rows.shape[0]
    heads = step_weight.shape[2]
    inputs_f = rows.astype(F32)
    scale = lax.rsqrt(jnp.mean(inputs_f * inputs_f, axis=1, keepdims=True) + EPS)
    normed = (inputs_f * scale * norm_gain[0]).astype(BF16)
    first = jnp.dot(
        normed,
        lax.all_gather(state_weight, "ctx", axis=1, tiled=True)[0],
        preferred_element_type=F32,
    )
    second = jnp.dot(
        normed,
        lax.all_gather(step_weight, "ctx", axis=1, tiled=True)[0],
        preferred_element_type=F32,
    )
    b_rows = first[:, :STATE].astype(BF16)
    c_rows = first[:, STATE:].astype(BF16)
    step_size = jax.nn.softplus(second + step_bias[0])
    log_decay = -step_size * jnp.exp(decay_log[0])
    heads_x = normed.reshape(count, heads, HEAD_DIM)
    causal = jnp.arange(count)[:, None] >= jnp.arange(count)[None, :]
    cumulative = jnp.dot(causal.astype(F32), log_decay, precision=lax.Precision.HIGHEST)
    by_head = cumulative.T
    gap = by_head[:, :, None] - by_head[:, None, :]
    factor = jnp.where(causal[None], jnp.exp(jnp.where(causal[None], gap, 0.0)), 0.0)
    scores = jnp.dot(c_rows, b_rows.T, preferred_element_type=F32)
    mixing = (factor * scores[None] * step_size.T[:, None, :]).astype(BF16)
    intra = jnp.einsum("hts,shp->thp", mixing, heads_x, preferred_element_type=F32)
    tail = jnp.exp(cumulative[-1][None, :] - cumulative) * step_size
    weighted = (heads_x.astype(F32) * tail[:, :, None]).astype(BF16)
    block_state = jnp.einsum("shp,sn->hpn", weighted, b_rows, preferred_element_type=F32)
    carry_full = lax.all_gather(carry_state[0].astype(BF16), "ctx", axis=0, tiled=True).astype(F32)
    identity = (jnp.zeros((heads,), F32), jnp.zeros(block_state.shape, F32))
    prefix_decay, prefix_state = entering(
        (cumulative[-1], block_state), "ctx", combine_states, identity
    )
    start = jnp.exp(prefix_decay)[:, None, None] * carry_full + prefix_state
    inter = jnp.exp(cumulative)[:, :, None] * jnp.einsum(
        "tn,hpn->thp", c_rows, start.astype(BF16), preferred_element_type=F32
    )
    mixed = intra + inter + skip_gain[0][None, :, None] * heads_x.astype(F32)
    output = (inputs_f + mixed.reshape(count, heads * HEAD_DIM)).astype(BF16)
    sections = lax.axis_size("section")
    route = [(i, (i + 1) % sections) for i in range(sections)]
    return lax.ppermute(output[None], "section", route)


def params():
    return pltpu.CompilerParams(vmem_limit_bytes=VMEM_LIMIT)


def call(kernel, name, outs, scratch=(), where=pltpu.VMEM, source=pltpu.VMEM, flops=0, aliases={}):
    def run(me, *arrays):
        results = pl.pallas_call(
            kernel,
            out_shape=[jax.ShapeDtypeStruct(*o) for o in outs],
            in_specs=[pl.BlockSpec(memory_space=pltpu.SMEM)]
            + [pl.BlockSpec(memory_space=source)] * len(arrays),
            out_specs=[pl.BlockSpec(memory_space=where)] * len(outs),
            scratch_shapes=scratch,
            compiler_params=params(),
            input_output_aliases=aliases,
            cost_estimate=pl.CostEstimate(
                flops=flops,
                transcendentals=0,
                bytes_accessed=sum(a.size * a.dtype.itemsize for a in arrays)
                + sum(math.prod(shape) * jnp.dtype(kind).itemsize for shape, kind in outs),
            ),
            name=name,
        )(me, *arrays)
        return list(results)

    return run


def split_kernel(which, me_ref, x_ref, *refs):
    outs, sems = refs[-1 - len(which) : -1], refs[-1]
    count, columns = outs[0].shape
    me = me_ref[0]
    copies = []
    for i, (d, out) in enumerate(zip(which, outs)):
        at = pl.multiple_of(lax.bitwise_xor(me, d) * columns, 128)
        for k in range(CUTS):
            part = slice(k * count // CUTS, (k + 1) * count // CUTS)
            copies.append(
                pltpu.make_async_copy(
                    x_ref.at[part, pl.ds(at, columns)], out.at[part], sems.at[i * CUTS + k]
                )
            )
    for copy in copies:
        copy.start()
    for copy in copies:
        copy.wait()


def join_kernel(which, me_ref, *refs):
    parts, out, sems = refs[: len(which)], refs[-2], refs[-1]
    count, columns = parts[0].shape
    me = me_ref[0]
    copies = []
    for i, (d, block) in enumerate(zip(which, parts)):
        at = pl.multiple_of(lax.bitwise_xor(me, d) * columns, 128)
        for k in range(CUTS):
            part = slice(k * count // CUTS, (k + 1) * count // CUTS)
            copies.append(
                pltpu.make_async_copy(
                    block.at[part], out.at[part, pl.ds(at, columns)], sems.at[i * CUTS + k]
                )
            )
    for copy in copies:
        copy.start()
    for copy in copies:
        copy.wait()


def lanes_of(shape):
    return lax.broadcasted_iota(jnp.int32, shape, 1)


def partial_kernel(heads, _, x_ref, gain_ref, w_ref, ws_ref, out_ref):
    x = x_ref[...].astype(F32)
    squares = jnp.sum(x * x, axis=1, keepdims=True)
    high = squares.astype(BF16).astype(F32)
    scaled = (x * gain_ref[...]).astype(BF16)
    rows = jnp.dot(scaled, w_ref[...], preferred_element_type=F32)
    raw = lax.dot_general(scaled, ws_ref[...], (((1,), (1,)), ((), ())), preferred_element_type=F32)
    lane = lanes_of(raw.shape)
    raw = jnp.where(lane == heads, high, raw)
    raw = jnp.where(lane == heads + 1, squares - high, raw)
    out_ref[:, : 2 * STATE] = rows.astype(BF16)
    out_ref[:, 2 * STATE :] = raw.astype(BF16)


def total_kernel(
    heads, width, me_ref, p0, p1, p2, p3, bias_ref, o0, o1, o2, o3, turned
):
    count = p0.shape[0]
    me = me_ref[0]
    total = sum(p[...].astype(F32) for p in (p0, p1, p2, p3))
    rows, raw = total[:, : 2 * STATE], total[:, 2 * STATE :]
    lane = lanes_of(raw.shape)
    squares = raw[:, heads : heads + 1] + raw[:, heads + 1 : heads + 2]
    scale = lax.rsqrt(jnp.broadcast_to(squares, raw.shape) * (1.0 / width) + EPS)
    biased = raw * scale + bias_ref[...]
    step = jnp.maximum(biased, 0.0) + jnp.log1p(jnp.exp(-jnp.abs(biased)))
    step = jnp.where(lane % GROUP == heads, scale, step)
    step = jnp.where(lane % GROUP > heads, 0.0, step)
    by_head = step.T
    high = by_head.astype(BF16)
    turned[:, :count] = high
    turned[:, count:] = (by_head - high.astype(F32)).astype(BF16)
    both = jnp.concatenate(
        [(rows[:, :STATE] * scale).T, rows[:, STATE:] * scale], axis=1
    ).astype(BF16)
    for d, out in enumerate((o0, o1, o2, o3)):
        put(me, d, both, turned, out)


def put(me, d, both, turned, out):
    count = both.shape[0]
    at = pl.multiple_of(lax.bitwise_xor(me, d) * GROUP, GROUP)
    out[:count, :] = both
    out[count:, :] = turned[pl.ds(at, GROUP), :]


def pieces(values, e, lane):
    values = pltpu.roll(values, -e * GROUP % 128, 1) if e else values
    high = values.astype(BF16).astype(F32)
    low = pltpu.roll(values - high, GROUP, 1)
    return jnp.where(lane < GROUP, high, jnp.where(lane < 2 * GROUP, low, 0.0)).astype(BF16)


def decays_of(heads, payloads, rate_ref, cum_ref, cumt_ref, stept_ref):
    count = cum_ref.shape[0]
    lane = lanes_of((count, 128))
    rows = [p[count:, :count].astype(F32) + p[count:, count:].astype(F32) for p in payloads]
    rest = [jnp.zeros((128 - 2 * GROUP, count), F32)]
    step = jnp.concatenate(rows + rest).T
    by_head = jnp.concatenate([r * r[heads : heads + 1, :] for r in rows] + rest)
    stept_ref[...] = by_head
    cum = jnp.dot(
        lower_half(count).astype(F32),
        step * rate_ref[...],
        precision=lax.Precision.HIGHEST,
        preferred_element_type=F32,
    )
    cum_ref[...] = jnp.where(lane % GROUP == heads, step, cum)
    cumt_ref[...] = cum.T
    last = cum[count - 1 : count, :]
    return jnp.exp(last - cum) * by_head.T, jnp.exp(last)


def lower_half(count):
    return lax.broadcasted_iota(jnp.int32, (count, count), 0) >= lax.broadcasted_iota(
        jnp.int32, (count, count), 1
    )


def block_states(x, payloads, tail, decay, spread_ref, made, kept):
    count, columns = x[0].shape
    lane = lanes_of((count, 128))
    decays = jnp.broadcast_to(decay, (8, 128))
    terms = jnp.concatenate(
        [pieces(tail, i, lane) for i in range(2)] + [pieces(decays, i, lane[:8]) for i in range(2)]
    )
    for j in range(0, columns, 256):
        at = slice(j, j + 256)
        wide = jnp.dot(terms, spread_ref[:, at], preferred_element_type=F32)
        for i in range(2):
            weighted = x[i][:, at].astype(F32) * wide[i * count : (i + 1) * count]
            kept[i][:, at] = wide[2 * count + 8 * i : 2 * count + 8 * (i + 1)]
            made[i][:, at] = jnp.dot(
                payloads[i][:count, :STATE], weighted.astype(BF16), preferred_element_type=F32
            )


def within_block(heads, i, x_ref, payload_ref, cum_ref, cumt_ref, stept_ref, gain_ref, skip_ref):
    count, columns = x_ref.shape
    lane = lanes_of((count, 128))
    cum = cum_ref[...]
    at = i * GROUP + heads
    scale = jnp.broadcast_to(cum[:, at : at + 1], (count, 128))
    lower = lower_half(count)
    scores = jnp.dot(
        payload_ref[:count, STATE:], payload_ref[:count, :STATE], preferred_element_type=F32
    )
    scores = jnp.where(lower, scores, 0.0)
    for j in range(columns // 128):
        at = slice(j * 128, (j + 1) * 128)
        low = x_ref[:, at]
        x = low.astype(F32)
        mixing, spread = [], []
        for k in range(2):
            row = i * GROUP + 2 * j + k
            gap = cum[:, row : row + 1] - cumt_ref[row : row + 1, :]
            factor = jnp.exp(jnp.where(lower, gap, 0.0))
            mixing.append((factor * scores * stept_ref[row : row + 1, :]).astype(BF16))
            mine = (lane < HEAD_DIM) if k == 0 else (lane >= HEAD_DIM)
            spread.append(jnp.where(mine, low, jnp.zeros_like(low)))
        intra = jnp.dot(
            jnp.concatenate(mixing, axis=1),
            jnp.concatenate(spread, axis=0),
            preferred_element_type=F32,
        )
        gain = gain_ref[:, at]
        yield at, x + (gain * intra + (skip_ref[:, at] * gain) * (x * scale))


def output_kernel(
    heads, e, i, _, x_ref, payload_ref, cum_ref, cumt_ref, stept_ref, start_ref, gain_ref, skip_ref,
    spread_ref, out_ref,
):
    count = x_ref.shape[0]
    grown = jnp.exp(cum_ref[...])
    grown = jnp.dot(
        pieces(grown, i, lanes_of(grown.shape)), spread_ref[...], preferred_element_type=F32
    )
    for at, inside in within_block(
        heads, i, x_ref, payload_ref, cum_ref, cumt_ref, stept_ref, gain_ref, skip_ref
    ):
        inter = jnp.dot(
            payload_ref[:count, STATE:], start_ref[e, :, at], preferred_element_type=F32
        )
        out_ref[:, at] = (inside + grown[:, at] * inter).astype(BF16)


def early_kernel(
    heads, _, x0, x3, p0, p3, gain_ref, rate_ref, skip_ref, spread_ref,
    cum_ref, cumt_ref, stept_ref, m0, m3, k0, k3, inside_ref, grown_ref,
):
    tail, decay = decays_of(heads, (p0, p3), rate_ref, cum_ref, cumt_ref, stept_ref)
    block_states((x0, x3), (p0, p3), tail, decay, spread_ref, (m0, m3), (k0, k3))
    grown = jnp.exp(cum_ref[...])
    grown_ref[...] = jnp.dot(
        pieces(grown, 1, lanes_of(grown.shape)), spread_ref[...], preferred_element_type=F32
    )
    for at, inside in within_block(
        heads, 1, x3, p3, cum_ref, cumt_ref, stept_ref, gain_ref, skip_ref
    ):
        inside_ref[:, at] = inside


def first_kernel(
    heads, me_ref, x1, x2, p1, p2, p3, m0, m3, k0, k3, inside_ref, grown_ref, gain_ref, rate_ref,
    carry_ref, spread_ref, cum_ref, cumt_ref, stept_ref, start_ref, out_ref, m1, m2, k1, k2,
):
    count, columns = x1.shape
    tail, decay = decays_of(heads, (p1, p2), rate_ref, cum_ref, cumt_ref, stept_ref)
    block_states((x1, x2), (p1, p2), tail, decay, spread_ref, (m1, m2), (k1, k2))
    made, kept = (m0, m1, m2, m3), (k0, k1, k2, k3)

    def follow(me):
        for j in range(columns // 128):
            at = slice(j * 128, (j + 1) * 128)
            state = carry_ref[:, at]
            for t in range(4):
                start_ref[t ^ me, :, at] = state.astype(BF16)
                if t < 3:
                    state = kept[t ^ me][0:1, at] * state + gain_ref[:, at] * made[t ^ me][:, at]

    for me in range(4):
        pl.when(me_ref[0] == me)(functools.partial(follow, me))
    for j in range(0, columns, 256):
        at = slice(j, j + 256)
        inter = jnp.dot(p3[:count, STATE:], start_ref[3, :, at], preferred_element_type=F32)
        out_ref[:, at] = (inside_ref[:, at] + grown_ref[:, at] * inter).astype(BF16)


def by_heads(
    activations, norm_gain, state_weight, step_weight, step_bias, decay_log, skip_gain, carry_state
):
    rows = activations[0]
    count, width = rows.shape
    heads = carry_state.shape[1]
    columns = heads * HEAD_DIM
    here = lax.axis_index("ctx")
    me = here.astype(jnp.int32).reshape(1)
    sections = lax.axis_size("section")
    block = ((count, columns), BF16)

    x = [None] * 4
    source = pltpu.with_memory_space_constraint(rows, pltpu.HBM)
    before = []
    for which in SPLITS:
        made = call(
            functools.partial(split_kernel, which),
            "split_" + "".join(map(str, which)),
            [block] * len(which),
            [pltpu.SemaphoreType.DMA((len(which) * CUTS,))],
            source=pl.ANY,
        )(me, source, *before)
        for d, part in zip(which, made):
            x[d] = part
        before = made[:1]
    for d in EXCHANGES:
        x[d] = lax.ppermute(x[d], "ctx", [(i, i ^ d) for i in range(4)])

    grouped = lambda a: jnp.pad(
        a.reshape(4, heads, -1), ((0, 0), (0, GROUP - heads), (0, 0))
    ).reshape(4 * GROUP, -1)
    ours = lambda a: lax.dynamic_slice_in_dim(a, here * heads, heads, 1)
    gain = lax.dynamic_slice_in_dim(norm_gain, here * columns, columns, 1)
    steps_by_head = grouped(step_weight[0].T)
    shares = [None] * 4
    for d in (0, *EXCHANGES):
        [shares[d]] = call(
            functools.partial(partial_kernel, heads),
            f"partial_{d}",
            [((count, 2 * STATE + 4 * GROUP), BF16)],
        )(me, x[d], gain, state_weight[0], steps_by_head)
        if d:
            shares[d] = lax.ppermute(shares[d], "ctx", [(i, i ^ d) for i in range(4)])
    payload = ((count + GROUP, 2 * STATE), BF16)
    payloads = [None] * 4
    payloads = call(
        functools.partial(total_kernel, heads, width),
        "total",
        [payload] * 4,
        [pltpu.VMEM((4 * GROUP, 2 * count), BF16)],
    )(me, *shares, grouped(step_bias[0]).T)
    for d in EXCHANGES:
        payloads[d] = lax.ppermute(payloads[d], "ctx", [(i, i ^ d) for i in range(4)])

    rate = jnp.tile(
        jnp.pad(-jnp.exp(ours(decay_log)), ((0, 0), (0, GROUP - heads))), (1, 4)
    )
    skip = jnp.repeat(ours(skip_gain), HEAD_DIM, axis=1)
    carry = carry_state[0].reshape(columns, STATE).T
    row = lax.broadcasted_iota(jnp.int32, (128, columns), 0)
    head = lax.broadcasted_iota(jnp.int32, (128, columns), 1) // HEAD_DIM
    spread = ((row % GROUP == head) & (row < 2 * GROUP)).astype(BF16)
    decays = [((count, 128), F32), ((128, count), F32), ((128, count), F32)]
    state, left, whole = ((STATE, columns), F32), ((8, columns), F32), ((count, columns), F32)
    *early, m0, m3, k0, k3, inside, grown = call(
        functools.partial(early_kernel, heads),
        "early",
        [*decays, state, state, left, left, whole, whole],
    )(me, x[0], x[3], payloads[0], payloads[3], gain, rate, skip, spread)
    *late, start, first = call(
        functools.partial(first_kernel, heads),
        "first",
        [*decays, ((4, STATE, columns), BF16), block],
        [pltpu.VMEM(*shape) for shape in (state, state, left, left)],
    )(me, *x[1:3], *payloads[1:], m0, m3, k0, k3, inside, grown, gain, rate, carry, spread)
    timed = {0: (0, early), 1: (0, late), 2: (1, late)}

    parts = [None] * 4
    for d in ORDER:
        part = first
        if d != ORDER[0]:
            i, made = timed[d]
            [part] = call(
                functools.partial(output_kernel, heads, d, i), f"output_{d}", [block]
            )(me, x[d], payloads[d], *made, start, gain, skip, spread)
        route = [
            (s * 4 + c, ((s + 1) % sections) * 4 + (c ^ d))
            for s in range(sections)
            for c in range(4)
        ]
        parts[d] = lax.ppermute(part, ("section", "ctx"), route)
    output = []
    for which in JOINS:
        output = call(
            functools.partial(join_kernel, which),
            "join_" + "".join(map(str, which)),
            [((count, width), BF16)],
            [pltpu.SemaphoreType.DMA((len(which) * CUTS,))],
            where=pl.ANY,
            source=pl.ANY,
            aliases={1 + len(which): 0} if output else {},
        )(me, *[parts[d] for d in which], *output)
    return output[0][None]


def per_device(*arguments):
    activations, carry_state = arguments[0], arguments[-1]
    heads, dim, state = carry_state.shape[1:]
    fits = (
        lax.axis_size("ctx") == 4
        and activations.shape[1] == 128
        and (dim, state) == (HEAD_DIM, STATE)
        and heads % 2 == 0
        and heads < GROUP
    )
    return (by_heads if fits else by_positions)(*arguments)


def solution(mesh):
    placed = (
        P("section", "ctx", None),
        P("section", None),
        P("section", "ctx", None),
        P("section", "ctx", None),
        P("section", None),
        P("section", None),
        P("section", None),
        P("section", "ctx", None, None),
    )
    return jax.shard_map(
        per_device, mesh=mesh, in_specs=placed, out_specs=P("section", "ctx", None), check_vma=False
    )
```
